32 devices in a mesh: row: 16 (over z, y, core), col: 2 (over x).
Axes of the slice: x: 2, y: 2, z: 4, core: 2. Of those that a mesh axis runs over, the one named last changes fastest.
Arguments:
- views: bfloat16 [81, 1024, 512], P(None, 'row', 'col'), may hold values from -6 to 6
Outputs:
- increment: float32 [1024, 512], P('row', 'col')
- residual: float32 [1024, 512], P('row', 'col')
The draws below stay inside these ranges and needn't reach their ends.
All inputs are finite; a program needn't handle non-finite values.
Results may differ from the reference program's by a relative error of at most 0.0005.
Values may be sent and summed in bfloat16 or wider, within the bound.
A program may use at most 64 MiB of HBM per device.

```python
import jax
import jax.numpy as jnp

ANG = 9
VIEWS = 81
D0 = 3
HALO = 13
ITERS = 2
NR = 1024
NC = 512


def levels(own_key, extent, split, least, high):
    factor_of = 1.0
    for axis_at, shards_of in split:
        draws = jax.random.uniform(jax.random.fold_in(jax.random.fold_in(own_key, 6), axis_at), (shards_of,), jnp.float32, least / len(split), high / len(split))
        factor_of = factor_of * jnp.repeat(jnp.exp(draws), extent[axis_at] // shards_of).reshape((-1,) + (1,) * (len(extent) - 1 - axis_at))
    return factor_of


def scatter_about(own_key, dims, scale, most, cuts=(), kind=jnp.bfloat16):
    loudness = levels(own_key, dims, cuts, -0.22, 0.18) if cuts else 1.0
    result = jax.random.normal(own_key, dims, jnp.float32) * scale * loudness
    return jnp.minimum(jnp.maximum(result, -most), most).astype(kind)


def setup_inputs(seed: int = 0) -> dict:
    key_of = jax.random.split(jax.random.key(seed), 2)
    views = scatter_about(key_of[0], (VIEWS, NR, NC), 1.0, 6.0, ((1, 16), (2, 2)))
    return {"views": views}


smooth_weight = 2.0
damping = 0.1

def edge_weights(center):
    padded = jnp.pad(center, 1)
    across = padded[1:-1, 1:] - padded[1:-1, :-1]
    vertical = padded[1:, 1:-1] - padded[:-1, 1:-1]
    columns = jnp.arange(NC + 1)
    row_index = jnp.arange(NR + 1)
    horiz = jnp.where(((columns >= 1) & (columns <= NC - 1))[None, :], jnp.exp(-across * across), 0.0)
    verti = jnp.where(((row_index >= 1) & (row_index <= NR - 1))[:, None], jnp.exp(-vertical * vertical), 0.0)
    return (horiz, verti)

def apply_operator(field, coeff, horiz, verti):
    padded = jnp.pad(field, 1)
    edges = horiz[:, 1:] * (field - padded[1:-1, 2:]) + horiz[:, :-1] * (field - padded[1:-1, :-2])
    edges = edges + verti[1:] * (field - padded[2:, 1:-1]) + verti[:-1] * (field - padded[:-2, 1:-1])
    return coeff * field + smooth_weight * edges

def reference(views):
    padded = jnp.pad(views, ((0, 0), (HALO, HALO), (HALO, HALO)))
    center = views[VIEWS // 2].astype(jnp.float32)
    data_sum = jnp.zeros((NR, NC), jnp.float32)
    source_sum = jnp.zeros((NR, NC), jnp.float32)
    for index in range(VIEWS):
        srow = index // ANG - ANG // 2
        tcol = index % ANG - ANG // 2
        top = HALO + D0 * srow
        left = HALO + D0 * tcol
        image = padded[index].astype(jnp.float32)
        warped = image[top:top + NR, left:left + NC]
        down_diff = 0.5 * (image[top + 1:top + 1 + NR, left:left + NC] - image[top - 1:top - 1 + NR, left:left + NC])
        side_diff = 0.5 * (image[top:top + NR, left + 1:left + 1 + NC] - image[top:top + NR, left - 1:left - 1 + NC])
        slope = srow * down_diff + tcol * side_diff
        error = warped - center
        robust = 1.0 / jnp.sqrt(1.0 + error * error)
        data_sum = data_sum + robust * slope * slope
        source_sum = source_sum - robust * slope * error
    coeff = damping + data_sum / VIEWS
    source = source_sum / VIEWS
    horiz, verti = edge_weights(center)
    precond = coeff + smooth_weight * (horiz[:, 1:] + horiz[:, :-1] + verti[1:] + verti[:-1])
    solution = jnp.zeros_like(source)
    residual = source
    zed = residual / precond
    direction = zed
    inner_now = jnp.sum(residual * zed)
    for step in range(ITERS):
        image_dir = apply_operator(direction, coeff, horiz, verti)
        step_size = inner_now / jnp.sum(direction * image_dir)
        solution = solution + step_size * direction
        residual = residual - step_size * image_dir
        zed = residual / precond
        inner_next = jnp.sum(residual * zed)
        direction = zed + inner_next / inner_now * direction
        inner_now = inner_next
    return (solution, residual)
```

```python
import functools

import jax
import jax.numpy as jnp
from jax import lax
from jax.experimental import pallas as pl
from jax.experimental.pallas import tpu as pltpu
from jax.sharding import PartitionSpec as P

ANG = 9
VIEWS = 81
HALF = 4
CENTER = 40
D0 = 3
smooth_weight = 2.0
damping = 0.1
PAD = 16
LANES = 128
F32 = jnp.float32
DIRS = ((-1, 0), (1, 0), (0, -1), (0, 1), (-1, -1), (-1, 1), (1, -1), (1, 1))


def roll(x, shift):
    return pltpu.roll(x, shift % LANES, 1)


def lane_of(rows):
    return lax.broadcasted_iota(jnp.int32, (rows, LANES), 1)


def kernel(nrow, ncol, views, out, ext, sp, col_r, col_l, fb, sb, band, pb, cen, cpack, acc, pacc, own, zc, gpack,
           ghost_u, ghost_d, ghost_l, ghost_r, corner, redbuf, redout, load_sem, send1, recv1, send2, recv2, rsend, rrecv, known):
    rows, cols = views.shape[1], views.shape[2]
    r, c = lax.axis_index("row"), lax.axis_index("col")
    count = nrow * ncol
    me = r * ncol + c
    full = PAD + rows + PAD

    def exists(dr, dc):
        return (r + dr >= 0) & (r + dr < nrow) & (c + dc >= 0) & (c + dc < ncol)

    barrier = pltpu.get_barrier_semaphore()

    def greet(sem, far):
        for dr, dc in DIRS:
            if abs(dr) * far < nrow and abs(dc) * far < ncol:
                @pl.when(exists(dr * far, dc * far))
                def _():
                    pl.semaphore_signal(sem, inc=1, device_id=(r + dr * far, c + dc * far), device_id_type=pl.DeviceIdType.MESH)

    def met(sem, far):
        total = 0
        for dr, dc in DIRS:
            if abs(dr) * far < nrow and abs(dc) * far < ncol:
                total = total + jnp.where(exists(dr * far, dc * far), 1, 0)
        pl.semaphore_wait(sem, total)

    greet(barrier, 1)
    reaches = []
    while 1 << len(reaches) < max(nrow, ncol) - 1:
        reaches.append(1 << len(reaches))

    def learn(step):
        if 0 < step <= len(reaches):
            met(known.at[step - 1], reaches[step - 1])
        if step < len(reaches):
            greet(known.at[step], reaches[step])

    loads = []
    for si in range(ANG):
        part = pl.ds(si * ANG, ANG)
        copy = pltpu.make_async_copy(views.at[part], ext.at[part, pl.ds(PAD, rows), :], load_sem.at[si])
        copy.start()
        loads.append(copy)

    def zero(ref, first, number, row, size):
        def body(i, carry):
            ref[first + i, row : row + size, :] = jnp.zeros((size, ref.shape[2]), ref.dtype)
            return carry
        lax.fori_loop(0, number, body, 0)

    @pl.when(r == 0)
    def _():
        zero(ext, 0, 41, 0, PAD)

    @pl.when(r == nrow - 1)
    def _():
        zero(ext, 40, 41, PAD + rows, PAD)

    for ref, edge in ((col_r, c == ncol - 1), (col_l, c == 0)):
        @pl.when(edge)
        def _():
            zero(ref, 0, 5, PAD, rows)

        @pl.when(edge | (r == 0))
        def _():
            zero(ref, 0, 3, 0, PAD)

        @pl.when(edge | (r == nrow - 1))
        def _():
            zero(ref, 2, 3, PAD + rows, PAD)

    for edge, ref in ((r == 0, ghost_u), (r == nrow - 1, ghost_d)):
        @pl.when(edge)
        def _():
            ref[0] = jnp.zeros((8, cols), F32)
            ref[1] = jnp.ones((8, cols), F32)
    for edge, ref, low in ((c == 0, ghost_l, 1.0), (c == ncol - 1, ghost_r, 0.0)):
        @pl.when(edge)
        def _():
            ref[...] = jnp.where(lane_of(rows) < 64, low, 1.0 - low)
    for index, (dr, dc) in enumerate(DIRS[4:]):
        @pl.when(jnp.logical_not(exists(-dr, -dc)))
        def _():
            corner[index] = jnp.zeros((8, LANES), F32)


    row_copies = []
    for size in range(HALF + 1):
        reach = 8 if D0 * size + 1 <= 8 else PAD
        for index, (dr, dc) in enumerate(DIRS[:2]):
            if size == 0:
                part = pl.ds(CENTER, 1)
            else:
                part = pl.ds(ANG * (HALF - dr * size), ANG)
            if dr < 0:
                src, dst = views.at[part, pl.ds(0, reach), :], ext.at[part, pl.ds(PAD + rows, reach), :]
            else:
                src, dst = views.at[part, pl.ds(rows - reach, reach), :], ext.at[part, pl.ds(PAD - reach, reach), :]
            row_copies.append((dr, dc, pltpu.make_async_remote_copy(
                src_ref=src, dst_ref=dst, send_sem=send1.at[2 * size + index], recv_sem=recv1.at[2 * size + index],
                device_id=(r + dr, c + dc), device_id_type=pl.DeviceIdType.MESH)))
    col_copies = []
    for index, (dr, dc) in enumerate(DIRS[2:]):
        side = col_r if dc < 0 else col_l
        mine = sp.at[0 if dc < 0 else 1]
        if dr == 0:
            src, dst = mine, side.at[:, pl.ds(PAD, rows), :]
        elif dr < 0:
            src, dst = mine.at[pl.ds(2, 3), pl.ds(0, PAD), :], side.at[pl.ds(2, 3), pl.ds(PAD + rows, PAD), :]
        else:
            src, dst = mine.at[pl.ds(0, 3), pl.ds(rows - PAD, PAD), :], side.at[pl.ds(0, 3), pl.ds(0, PAD), :]
        col_copies.append((dr, dc, pltpu.make_async_remote_copy(
            src_ref=src, dst_ref=dst, send_sem=send1.at[10 + index], recv_sem=recv1.at[10 + index],
            device_id=(r + dr, c + dc), device_id_type=pl.DeviceIdType.MESH)))

    def start(group):
        for dr, dc, copy in group:
            @pl.when(exists(dr, dc))
            def _():
                copy.start()

    def arrive(group):
        for dr, dc, copy in group:
            @pl.when(exists(-dr, -dc))
            def _():
                copy.wait_recv()

    def drain(group):
        for dr, dc, copy in group:
            @pl.when(exists(dr, dc))
            def _():
                copy.wait_send()

    offset = lax.broadcasted_iota(jnp.int32, (cols, cols), 0) - lax.broadcasted_iota(jnp.int32, (cols, cols), 1)
    plain = jnp.where(offset == 1, 1.0, jnp.where(offset == -1, -1.0, 0.0))
    for ti in range(ANG):
        band[ti] = (plain * float(ti - HALF)).astype(band.dtype)

    met(barrier, 1)
    start(row_copies)
    learn(0)
    for copy in loads:
        copy.wait()

    lane = lane_of(rows)
    group = (lane % 64) // 16
    place = lane % 16
    right_part = lane < 64

    for slot in range(5):
        left = right = None
        for half in range(2):
            if slot == 2 and half == 1:
                a = roll(ext[CENTER, PAD : PAD + rows, 0:LANES].astype(F32), 64)
                b = ext[CENTER, PAD : PAD + rows, cols - LANES : cols].astype(F32)
            else:
                si = (0, 2, 4, 5, 7)[slot] + half
                a = b = None
                for g in range(HALF):
                    x = ext[si * ANG + HALF + g + 1, PAD : PAD + rows, 0:LANES].astype(F32)
                    x = roll(x, 16 * g + 2 + 64 * half)
                    a = x if a is None else jnp.where(group == g, x, a)
                    x = ext[si * ANG + HALF - g - 1, PAD : PAD + rows, cols - LANES : cols].astype(F32)
                    x = roll(x, 16 * g + 14 + 64 * half)
                    b = x if b is None else jnp.where(group == g, x, b)
            left = a if half == 0 else jnp.where(right_part, left, a)
            right = b if half == 0 else jnp.where(right_part, right, b)
        sp[0, slot] = left.astype(sp.dtype)
        sp[1, slot] = right.astype(sp.dtype)
    start(col_copies)

    center = [ext[CENTER, PAD : PAD + rows, h * LANES : (h + 1) * LANES].astype(F32) for h in range(2)]
    ca, cb = center
    for ti in range(ANG):
        move = D0 * (ti - HALF)
        ra, rb = roll(ca, move), roll(cb, move)
        if move > 0:
            cen[ti, 0] = ra
            cen[ti, 1] = jnp.where(lane >= move, rb, ra)
        elif move < 0:
            cen[ti, 0] = jnp.where(lane < LANES + move, ra, rb)
            cen[ti, 1] = rb
        else:
            cen[ti, 0] = ca
            cen[ti, 1] = cb
    total = jnp.zeros((rows, LANES), F32)
    for g in range(HALF):
        m = D0 * (g + 1)
        total = jnp.where(right_part & (group == g), roll(cb, 16 * g - 126 + m), total)
        total = jnp.where((~right_part) & (group == g), roll(ca, 78 + 16 * g - m), total)
    cpack[...] = total
    pacc[...] = jnp.zeros_like(pacc)

    chunk = 16
    clane = lane_of(chunk)

    def terms(v0, side, down, s, middle):
        if s == 0:
            slope = side
        else:
            slope = side + (down if abs(s) == 1 else float(abs(s)) * down)
        error = v0 - middle
        weighted = slope * lax.rsqrt(1.0 + error * error)
        return weighted * slope, weighted * error

    def difference(ref, head, base, s):
        after, before = (base + 1, base - 1) if s > 0 else (base - 1, base + 1)
        return ref[head + (slice(after, after + chunk), slice(None))] - ref[head + (slice(before, before + chunk), slice(None))]

    def view_step(slot, s, at, middle, sums):
        base = PAD + D0 * s + at
        for h in range(2):
            v0, side = fb[slot, h, base : base + chunk, :], sb[slot, h, base : base + chunk, :]
            data, src = terms(v0, side, difference(fb, (slot, h), base, s) if s else None, s, middle[h])
            sums[0][h] = data if sums[0][h] is None else sums[0][h] + data
            sums[1][h] = src if sums[1][h] is None else sums[1][h] + src

    def widen(ti, slot, s, low, high):
        part = ext[ANG * (s + HALF) + ti, low:high, :]
        wide = part.astype(F32)
        side = jnp.dot(part, band[ti], preferred_element_type=F32)
        for h in range(2):
            fb[slot, h, low:high, :] = wide[:, h * LANES : (h + 1) * LANES]
            sb[slot, h, low:high, :] = side[:, h * LANES : (h + 1) * LANES]

    def needs_halo(s, at):
        return (s > 0 and at == rows - chunk) or (s < 0 and at == 0)

    def slot_of(ti, s):
        return (ti % 3) * ANG + s + HALF

    def inner_pass(ti):
        for s in range(-HALF, HALF + 1):
            widen(ti, slot_of(ti, s), s, PAD, PAD + rows)
        for at in range(0, rows, chunk):
            sums = [[None, None], [None, None]]
            middle = [cen[ti, h, at : at + chunk, :] for h in range(2)]
            for s in range(-HALF, HALF + 1):
                if not needs_halo(s, at):
                    view_step(slot_of(ti, s), s, at, middle, sums)
            for f in range(2):
                for h in range(2):
                    acc[ti, f, h, at : at + chunk, :] = sums[f][h]

    for ti in range(ANG):
        inner_pass(ti)
        if ti % 3 == 2:
            learn(ti // 3 + 1)
    arrive(row_copies[:2] + col_copies)
    frows, fcols = rows + 16, cols + 2 * LANES
    bands = []
    for part in (slice(0, PAD), slice(PAD, PAD + rows), slice(PAD + rows, full)):
        bands.append(jnp.concatenate([
            col_l[2, part, :].astype(F32), ext[CENTER, part, :].astype(F32), roll(col_r[2, part, :].astype(F32), 64)], axis=1))
    cf = jnp.concatenate([bands[0][8:16], bands[1], bands[2][0:8]], axis=0)
    gcol = lax.broadcasted_iota(jnp.int32, (frows, fcols), 1) + (c * cols - LANES)
    grow = lax.broadcasted_iota(jnp.int32, (frows, fcols), 0) + (r * rows - 8)

    def east(x):
        return pltpu.roll(x, fcols - 1, 1)

    def west(x):
        return pltpu.roll(x, 1, 1)

    def south(x):
        return pltpu.roll(x, frows - 1, 0)

    def north(x):
        return pltpu.roll(x, 1, 0)

    dx = east(cf) - cf
    dy = south(cf) - cf
    edge_e = jnp.where((gcol >= 0) & (gcol < ncol * cols - 1), smooth_weight * jnp.exp(-dx * dx), 0.0)
    edge_s = jnp.where((grow >= 0) & (grow < nrow * rows - 1), smooth_weight * jnp.exp(-dy * dy), 0.0)
    edge_w, edge_n = west(edge_e), north(edge_s)
    weights = edge_e + edge_w + edge_s + edge_n

    flane = lane_of(full)
    fgroup, fplace, fright = (flane % 64) // 16, flane % 16, flane < 64
    ptscale = jnp.where(clane < 64, 1.0, -1.0) * ((clane % 64) // 16 + 1).astype(F32)

    def packed_rows(si, low, high):
        slot, half = ((0, 0), (0, 1), (1, 0), (1, 1), (2, 0), (3, 0), (3, 1), (4, 0), (4, 1))[si]
        part = slice(low, high)
        right, grp, plc = fright[part], fgroup[part], fplace[part]
        x, z = col_r[slot, part, :].astype(F32), col_l[slot, part, :].astype(F32)
        merged = jnp.where(right, roll(x, 64) if half else x, z if half else roll(z, 64))
        for g in range(HALF):
            a = ext[si * ANG + HALF - g - 1, part, 0:LANES].astype(F32)
            b = ext[si * ANG + HALF + g + 1, part, cols - LANES : cols].astype(F32)
            merged = jnp.where(right & (grp == g) & (plc < 2), roll(b, 16 * g + 2), merged)
            merged = jnp.where((~right) & (grp == g) & (plc >= 14), roll(a, 16 * g + 78), merged)
        pb[si, part, :] = merged

    def packed_step(si, at):
        s = si - HALF
        base = PAD + D0 * s + at
        v0 = pb[si, base : base + chunk, :]
        side = ptscale * (roll(v0, -1) - roll(v0, 1))
        data, src = terms(v0, side, difference(pb, (si,), base, s) if s else None, s, cpack[at : at + chunk, :])
        pacc[0, at : at + chunk, :] += data
        pacc[1, at : at + chunk, :] += src

    def last_rows(si):
        return None if si == HALF else rows - chunk if si > HALF else 0

    for si in range(ANG):
        packed_rows(si, PAD, PAD + rows)
        for at in range(0, rows, chunk):
            if at != last_rows(si):
                packed_step(si, at)
    learn(4)

    def combine(low, high):
        part = slice(low, high)
        place_of = lane_of(high - low)
        for f in range(2):
            ta, tb = acc[HALF, f, 0, part, :], acc[HALF, f, 1, part, :]
            strip = pacc[f, part, :]
            for ti in range(ANG):
                m = D0 * abs(ti - HALF)
                if m == 0:
                    continue
                a, b = acc[ti, f, 0, part, :], acc[ti, f, 1, part, :]
                g = m // D0 - 1
                if ti > HALF:
                    ra, rb = roll(a, -m), roll(b, -m)
                    ta = ta + jnp.where(place_of < LANES - m, ra, rb)
                    tb = tb + jnp.where(place_of <= LANES - 2 - m, rb, roll(strip, 126 - m - 16 * g))
                else:
                    ra, rb = roll(a, m), roll(b, m)
                    ta = ta + jnp.where(place_of >= m + 1, ra, roll(strip, m - 78 - 16 * g))
                    tb = tb + jnp.where(place_of >= m, rb, ra)
            own[f, part, 0:LANES] = ta
            own[f, part, LANES : 2 * LANES] = tb

    def edge_size(size):
        for ti in range(ANG):
            for sign, at in ((1, rows - chunk), (-1, 0)):
                slot = 2 * ti + (sign < 0)
                low = PAD + at if sign > 0 else 0
                widen(ti, slot, sign * size, low, low + 2 * PAD)
            for sign, at in ((1, rows - chunk), (-1, 0)):
                slot = 2 * ti + (sign < 0)
                sums = [[acc[ti, f, h, at : at + chunk, :] for h in range(2)] for f in range(2)]
                middle = [cen[ti, h, at : at + chunk, :] for h in range(2)]
                view_step(slot, sign * size, at, middle, sums)
                for f in range(2):
                    for h in range(2):
                        acc[ti, f, h, at : at + chunk, :] = sums[f][h]
        for si in (HALF - size, HALF + size):
            low = PAD + rows if si > HALF else 0
            packed_rows(si, low, low + PAD)
            packed_step(si, last_rows(si))

    combine(chunk, rows - chunk)
    for size in range(1, HALF + 1):
        arrive(row_copies[2 * size : 2 * size + 2])
        edge_size(size)
    combine(0, chunk)
    combine(rows - chunk, rows)

    coeff = damping + own[0] * (0.25 / VIEWS)
    source = own[1] * (-0.5 / VIEWS)

    inner = (slice(8, 8 + rows), slice(LANES, LANES + cols))
    zed = source / (coeff + weights[inner])
    zc[0] = zed
    zc[1] = coeff
    gpack[0] = jnp.where(right_part, zed[:, 0:LANES], roll(coeff[:, 0:LANES], 64))
    gpack[1] = jnp.where(right_part, roll(coeff[:, cols - LANES : cols], 64), zed[:, cols - LANES : cols])

    copies2 = []
    for index, (dr, dc) in enumerate(DIRS):
        if dc == 0:
            src = zc.at[:, pl.ds(0, 8), :] if dr < 0 else zc.at[:, pl.ds(rows - 8, 8), :]
            dst = ghost_d if dr < 0 else ghost_u
        elif dr == 0:
            src = gpack.at[0] if dc < 0 else gpack.at[1]
            dst = ghost_r if dc < 0 else ghost_l
        else:
            src = gpack.at[0 if dc < 0 else 1, pl.ds(0 if dr < 0 else rows - 8, 8), :]
            dst = corner.at[index - 4]
        copies2.append((dr, dc, pltpu.make_async_remote_copy(
            src_ref=src, dst_ref=dst, send_sem=send2.at[index], recv_sem=recv2.at[index],
            device_id=(r + dr, c + dc), device_id_type=pl.DeviceIdType.MESH)))
    start(copies2)
    drain(row_copies + col_copies)
    for step in range(5, len(reaches) + 1):
        learn(step)
    arrive(copies2)

    zf = jnp.concatenate([
        jnp.concatenate([corner[3], ghost_u[0], corner[2]], axis=1),
        jnp.concatenate([ghost_l[...], zed, ghost_r[...]], axis=1),
        jnp.concatenate([corner[1], ghost_d[0], corner[0]], axis=1)], axis=0)
    one = jnp.ones((8, LANES), F32)
    kf = jnp.concatenate([
        jnp.concatenate([one, ghost_u[1], one], axis=1),
        jnp.concatenate([roll(ghost_l[...], 64), coeff, roll(ghost_r[...], 64)], axis=1),
        jnp.concatenate([one, ghost_d[1], one], axis=1)], axis=0)
    diag = kf + weights

    def gather(z):
        return edge_e * east(z) + edge_w * west(z) + edge_s * south(z) + edge_n * north(z)

    around = gather(zf)
    yf = around / diag
    n1, y = around[inner], yf[inner]
    n2 = gather(yf)[inner]
    w = source - n1
    q = zed - y
    wv = n1 - n2
    v = w - wv
    sums = (y * n1, q * n1, q * w, y * wv, y * v, q * v)
    line = lax.broadcasted_iota(jnp.int32, (1, LANES), 1)
    packed = jnp.zeros((1, LANES), F32)
    for i, x in enumerate(sums):
        x = jnp.sum(x, axis=0, keepdims=True)
        x = jnp.sum(x, axis=1, keepdims=True)
        packed = jnp.where(line == i, x, packed)
    redout[0] = packed
    redbuf[me] = packed

    def red_copy(i):
        peer = (me + i) % count
        return pltpu.make_async_remote_copy(
            src_ref=redout.at[0], dst_ref=redbuf.at[me], send_sem=rsend.at[0], recv_sem=rrecv.at[0],
            device_id=(peer // ncol, peer % ncol), device_id_type=pl.DeviceIdType.MESH)

    def cast_out(i, carry):
        red_copy(i).start()
        return carry

    lax.fori_loop(1, count, cast_out, 0)
    drain(copies2)
    others = redbuf.at[pl.ds(0, count - 1)]
    pltpu.make_async_copy(others, others, rrecv.at[0]).wait()
    pltpu.make_async_copy(others, others, rsend.at[0]).wait()
    totals = jnp.sum(redbuf[...], axis=0)
    f, g, h, k, l, m = [totals[:, i : i + 1] for i in range(6)]
    b, e = g + h, f + g
    delta = e / b
    step0 = (e + b) / b
    rz0 = e + b
    rz1 = f - 2.0 * delta * g + delta * delta * h
    wu1 = k - 2.0 * delta * l + delta * delta * m
    beta = rz1 / rz0
    step1 = rz1 / (wu1 - beta * rz1 / step0)
    direction = (y - delta * q) + beta * zed
    image = (wv - delta * v) + beta * w
    out[0] = step0 * zed + step1 * direction
    out[1] = (n1 - delta * w) - step1 * image


def solution(mesh):
    nrow, ncol = mesh.shape["row"], mesh.shape["col"]

    def shards(views):
        _, rows, cols = views.shape
        full = PAD + rows + PAD
        bf = views.dtype
        out = pl.pallas_call(
            functools.partial(kernel, nrow, ncol),
            out_shape=jax.ShapeDtypeStruct((2, rows, cols), F32),
            in_specs=[pl.BlockSpec(memory_space=pltpu.HBM)],
            out_specs=pl.BlockSpec(memory_space=pltpu.VMEM),
            scratch_shapes=[
                pltpu.VMEM((VIEWS, full, cols), bf),
                pltpu.VMEM((2, 5, rows, LANES), bf),
                pltpu.VMEM((5, full, LANES), bf),
                pltpu.VMEM((5, full, LANES), bf),
                pltpu.VMEM((3 * ANG, 2, full, LANES), F32),
                pltpu.VMEM((3 * ANG, 2, full, LANES), F32),
                pltpu.VMEM((ANG, cols, cols), bf),
                pltpu.VMEM((ANG, full, LANES), F32),
                pltpu.VMEM((ANG, 2, rows, LANES), F32),
                pltpu.VMEM((rows, LANES), F32),
                pltpu.VMEM((ANG, 2, 2, rows, LANES), F32),
                pltpu.VMEM((2, rows, LANES), F32),
                pltpu.VMEM((2, rows, cols), F32),
                pltpu.VMEM((2, rows, cols), F32),
                pltpu.VMEM((2, rows, LANES), F32),
                pltpu.VMEM((2, 8, cols), F32),
                pltpu.VMEM((2, 8, cols), F32),
                pltpu.VMEM((rows, LANES), F32),
                pltpu.VMEM((rows, LANES), F32),
                pltpu.VMEM((4, 8, LANES), F32),
                pltpu.VMEM((nrow * ncol, 1, LANES), F32),
                pltpu.VMEM((1, 1, LANES), F32),
                pltpu.SemaphoreType.DMA((ANG,)),
                pltpu.SemaphoreType.DMA((16,)),
                pltpu.SemaphoreType.DMA((16,)),
                pltpu.SemaphoreType.DMA((8,)),
                pltpu.SemaphoreType.DMA((8,)),
                pltpu.SemaphoreType.DMA((1,)),
                pltpu.SemaphoreType.DMA((1,)),
                pltpu.SemaphoreType.REGULAR((8,)),
            ],
            compiler_params=pltpu.CompilerParams(collective_id=0, has_side_effects=True, vmem_limit_bytes=48 << 20),
        )(pltpu.with_memory_space_constraint(views, pltpu.HBM))
        return out[0], out[1]

    return jax.shard_map(
        shards,
        mesh=mesh,
        in_specs=(P(None, "row", "col"),),
        out_specs=(P("row", "col"), P("row", "col")),
        check_vma=False,
    )
```

```python
import functools

import jax
import jax.numpy as jnp
from jax import lax
from jax.experimental import pallas as pl
from jax.experimental.pallas import tpu as pltpu
from jax.sharding import PartitionSpec as P

ANG = 9
VIEWS = 81
HALF = 4
CENTER = 40
D0 = 3
smooth_weight = 2.0
damping = 0.1
PAD = 16
GROUPS = ((1, 2, 3), (4,))
LANES = 128
F32 = jnp.float32
DIRS = ((-1, 0), (1, 0), (0, -1), (0, 1), (-1, -1), (-1, 1), (1, -1), (1, 1))


def roll(x, shift):
    return pltpu.roll(x, shift % LANES, 1)


def lane_of(rows):
    return lax.broadcasted_iota(jnp.int32, (rows, LANES), 1)


def kernel(nrow, ncol, views, out, ext, sp, col_r, col_l, fb, sb, band, pb, cen, cpack, acc, pacc, own, zc, gpack,
           ghost_u, ghost_d, ghost_l, ghost_r, corner, redbuf, redout, load_sem, send1, recv1, send2, recv2, rsend, rrecv, known):
    rows, cols = views.shape[1], views.shape[2]
    r, c = lax.axis_index("row"), lax.axis_index("col")
    count = nrow * ncol
    me = r * ncol + c
    full = PAD + rows + PAD

    def exists(dr, dc):
        return (r + dr >= 0) & (r + dr < nrow) & (c + dc >= 0) & (c + dc < ncol)

    barrier = pltpu.get_barrier_semaphore()

    def greet(sem, far):
        for dr, dc in DIRS:
            if abs(dr) * far < nrow and abs(dc) * far < ncol:
                @pl.when(exists(dr * far, dc * far))
                def _():
                    pl.semaphore_signal(sem, inc=1, device_id=(r + dr * far, c + dc * far), device_id_type=pl.DeviceIdType.MESH)

    def met(sem, far):
        total = 0
        for dr, dc in DIRS:
            if abs(dr) * far < nrow and abs(dc) * far < ncol:
                total = total + jnp.where(exists(dr * far, dc * far), 1, 0)
        pl.semaphore_wait(sem, total)

    greet(barrier, 1)
    reaches = []
    while 1 << len(reaches) < max(nrow, ncol) - 1:
        reaches.append(1 << len(reaches))

    def learn(step):
        if 0 < step <= len(reaches):
            met(known.at[step - 1], reaches[step - 1])
        if step < len(reaches):
            greet(known.at[step], reaches[step])

    loads = []
    for si in range(ANG):
        part = pl.ds(si * ANG, ANG)
        copy = pltpu.make_async_copy(views.at[part], ext.at[part, pl.ds(PAD, rows), :], load_sem.at[si])
        copy.start()
        loads.append(copy)

    def zero(ref, first, number, row, size):
        def body(i, carry):
            ref[first + i, row : row + size, :] = jnp.zeros((size, ref.shape[2]), ref.dtype)
            return carry
        lax.fori_loop(0, number, body, 0)

    @pl.when(r == 0)
    def _():
        zero(ext, 0, 41, 0, PAD)

    @pl.when(r == nrow - 1)
    def _():
        zero(ext, 40, 41, PAD + rows, PAD)

    for ref, edge in ((col_r, c == ncol - 1), (col_l, c == 0)):
        @pl.when(edge)
        def _():
            zero(ref, 0, 5, PAD, rows)

        @pl.when(edge | (r == 0))
        def _():
            zero(ref, 0, 3, 0, PAD)

        @pl.when(edge | (r == nrow - 1))
        def _():
            zero(ref, 2, 3, PAD + rows, PAD)

    for edge, ref in ((r == 0, ghost_u), (r == nrow - 1, ghost_d)):
        @pl.when(edge)
        def _():
            ref[0] = jnp.zeros((8, cols), F32)
            ref[1] = jnp.ones((8, cols), F32)
    for edge, ref, low in ((c == 0, ghost_l, 1.0), (c == ncol - 1, ghost_r, 0.0)):
        @pl.when(edge)
        def _():
            ref[...] = jnp.where(lane_of(rows) < 64, low, 1.0 - low)
    for index, (dr, dc) in enumerate(DIRS[4:]):
        @pl.when(jnp.logical_not(exists(-dr, -dc)))
        def _():
            corner[index] = jnp.zeros((8, LANES), F32)


    row_copies = []
    for size in range(HALF + 1):
        reach = 8 if D0 * size + 1 <= 8 else PAD
        for index, (dr, dc) in enumerate(DIRS[:2]):
            if size == 0:
                part = pl.ds(CENTER, 1)
            else:
                part = pl.ds(ANG * (HALF - dr * size), ANG)
            if dr < 0:
                src, dst = views.at[part, pl.ds(0, reach), :], ext.at[part, pl.ds(PAD + rows, reach), :]
            else:
                src, dst = views.at[part, pl.ds(rows - reach, reach), :], ext.at[part, pl.ds(PAD - reach, reach), :]
            row_copies.append((dr, dc, pltpu.make_async_remote_copy(
                src_ref=src, dst_ref=dst, send_sem=send1.at[2 * size + index], recv_sem=recv1.at[2 * size + index],
                device_id=(r + dr, c + dc), device_id_type=pl.DeviceIdType.MESH)))
    col_copies = []
    for index, (dr, dc) in enumerate(DIRS[2:]):
        side = col_r if dc < 0 else col_l
        mine = sp.at[0 if dc < 0 else 1]
        if dr == 0:
            src, dst = mine, side.at[:, pl.ds(PAD, rows), :]
        elif dr < 0:
            src, dst = mine.at[pl.ds(2, 3), pl.ds(0, PAD), :], side.at[pl.ds(2, 3), pl.ds(PAD + rows, PAD), :]
        else:
            src, dst = mine.at[pl.ds(0, 3), pl.ds(rows - PAD, PAD), :], side.at[pl.ds(0, 3), pl.ds(0, PAD), :]
        col_copies.append((dr, dc, pltpu.make_async_remote_copy(
            src_ref=src, dst_ref=dst, send_sem=send1.at[10 + index], recv_sem=recv1.at[10 + index],
            device_id=(r + dr, c + dc), device_id_type=pl.DeviceIdType.MESH)))

    def start(group):
        for dr, dc, copy in group:
            @pl.when(exists(dr, dc))
            def _():
                copy.start()

    def arrive(group):
        for dr, dc, copy in group:
            @pl.when(exists(-dr, -dc))
            def _():
                copy.wait_recv()

    def drain(group):
        for dr, dc, copy in group:
            @pl.when(exists(dr, dc))
            def _():
                copy.wait_send()

    offset = lax.broadcasted_iota(jnp.int32, (cols, cols), 0) - lax.broadcasted_iota(jnp.int32, (cols, cols), 1)
    plain = jnp.where(offset == 1, 1.0, jnp.where(offset == -1, -1.0, 0.0))
    for ti in range(ANG):
        band[ti] = (plain * float(ti - HALF)).astype(band.dtype)

    met(barrier, 1)
    start(row_copies)
    learn(0)
    for copy in loads:
        copy.wait()

    lane = lane_of(rows)
    group = (lane % 64) // 16
    place = lane % 16
    right_part = lane < 64

    for slot in range(5):
        left = right = None
        for half in range(2):
            if slot == 2 and half == 1:
                a = roll(ext[CENTER, PAD : PAD + rows, 0:LANES].astype(F32), 64)
                b = ext[CENTER, PAD : PAD + rows, cols - LANES : cols].astype(F32)
            else:
                si = (0, 2, 4, 5, 7)[slot] + half
                a = b = None
                for g in range(HALF):
                    x = ext[si * ANG + HALF + g + 1, PAD : PAD + rows, 0:LANES].astype(F32)
                    x = roll(x, 16 * g + 2 + 64 * half)
                    a = x if a is None else jnp.where(group == g, x, a)
                    x = ext[si * ANG + HALF - g - 1, PAD : PAD + rows, cols - LANES : cols].astype(F32)
                    x = roll(x, 16 * g + 14 + 64 * half)
                    b = x if b is None else jnp.where(group == g, x, b)
            left = a if half == 0 else jnp.where(right_part, left, a)
            right = b if half == 0 else jnp.where(right_part, right, b)
        sp[0, slot] = left.astype(sp.dtype)
        sp[1, slot] = right.astype(sp.dtype)
    start(col_copies)

    center = [ext[CENTER, PAD : PAD + rows, h * LANES : (h + 1) * LANES].astype(F32) for h in range(2)]
    ca, cb = center
    for ti in range(ANG):
        move = D0 * (ti - HALF)
        ra, rb = roll(ca, move), roll(cb, move)
        if move > 0:
            cen[ti, 0] = ra
            cen[ti, 1] = jnp.where(lane >= move, rb, ra)
        elif move < 0:
            cen[ti, 0] = jnp.where(lane < LANES + move, ra, rb)
            cen[ti, 1] = rb
        else:
            cen[ti, 0] = ca
            cen[ti, 1] = cb
    total = jnp.zeros((rows, LANES), F32)
    for g in range(HALF):
        m = D0 * (g + 1)
        total = jnp.where(right_part & (group == g), roll(cb, 16 * g - 126 + m), total)
        total = jnp.where((~right_part) & (group == g), roll(ca, 78 + 16 * g - m), total)
    cpack[...] = total
    pacc[...] = jnp.zeros_like(pacc)

    chunk = 8

    def terms(v0, side, down, s, middle):
        if s == 0:
            slope = side
        else:
            slope = side + (down if abs(s) == 1 else float(abs(s)) * down)
        error = v0 - middle
        weighted = slope * lax.rsqrt(1.0 + error * error)
        return weighted * slope, weighted * error

    def difference(ref, head, base, size, s):
        after, before = (base + 1, base - 1) if s > 0 else (base - 1, base + 1)
        return ref[head + (slice(after, after + size), slice(None))] - ref[head + (slice(before, before + size), slice(None))]

    def view_step(k, s, at, middle, sums):
        base = PAD + D0 * s + at
        for h in range(2):
            v0, side = fb[k, h, base : base + chunk, :], sb[k, h, base : base + chunk, :]
            data, src = terms(v0, side, difference(fb, (k, h), base, chunk, s) if s else None, s, middle[h])
            sums[0][h] = data if sums[0][h] is None else sums[0][h] + data
            sums[1][h] = src if sums[1][h] is None else sums[1][h] + src

    def widen(ti, spans):
        part = jnp.concatenate([ext[k, low:high, :] for k, low, high in spans], axis=0)
        wide = part.astype(F32)
        side = jnp.dot(part, band[ti], preferred_element_type=F32)
        first = 0
        for k, low, high in spans:
            rest = slice(first, first + high - low)
            for h in range(2):
                fb[k, h, low:high, :] = wide[rest, h * LANES : (h + 1) * LANES]
                sb[k, h, low:high, :] = side[rest, h * LANES : (h + 1) * LANES]
            first += high - low

    def view_of(ti, s):
        return ANG * (s + HALF) + ti

    def inner_rows(s):
        reach = -(-(D0 * abs(s) + 1) // chunk) * chunk if s else 0
        return (reach if s < 0 else 0), (rows - reach if s > 0 else rows)

    def inner_pass(ti):
        for s in range(-HALF, HALF + 1):
            widen(ti, [(view_of(ti, s), PAD, PAD + rows)])
        for at in range(0, rows, chunk):
            sums = [[None, None], [None, None]]
            middle = [cen[ti, h, at : at + chunk, :] for h in range(2)]
            for s in range(-HALF, HALF + 1):
                low, high = inner_rows(s)
                if low <= at < high:
                    view_step(view_of(ti, s), s, at, middle, sums)
            for f in range(2):
                for h in range(2):
                    acc[ti, f, h, at : at + chunk, :] = sums[f][h]

    for ti in range(ANG):
        inner_pass(ti)
        if ti % 3 == 2:
            learn(ti // 3 + 1)
    arrive(row_copies[:2] + col_copies)
    frows, fcols = rows + 16, cols + 2 * LANES
    bands = []
    for part in (slice(0, PAD), slice(PAD, PAD + rows), slice(PAD + rows, full)):
        bands.append(jnp.concatenate([
            col_l[2, part, :].astype(F32), ext[CENTER, part, :].astype(F32), roll(col_r[2, part, :].astype(F32), 64)], axis=1))
    cf = jnp.concatenate([bands[0][8:16], bands[1], bands[2][0:8]], axis=0)
    gcol = lax.broadcasted_iota(jnp.int32, (frows, fcols), 1) + (c * cols - LANES)
    grow = lax.broadcasted_iota(jnp.int32, (frows, fcols), 0) + (r * rows - 8)

    def east(x):
        return pltpu.roll(x, fcols - 1, 1)

    def west(x):
        return pltpu.roll(x, 1, 1)

    def south(x):
        return pltpu.roll(x, frows - 1, 0)

    def north(x):
        return pltpu.roll(x, 1, 0)

    dx = east(cf) - cf
    dy = south(cf) - cf
    edge_e = jnp.where((gcol >= 0) & (gcol < ncol * cols - 1), smooth_weight * jnp.exp(-dx * dx), 0.0)
    edge_s = jnp.where((grow >= 0) & (grow < nrow * rows - 1), smooth_weight * jnp.exp(-dy * dy), 0.0)
    edge_w, edge_n = west(edge_e), north(edge_s)
    weights = edge_e + edge_w + edge_s + edge_n

    flane = lane_of(full)
    fgroup, fplace, fright = (flane % 64) // 16, flane % 16, flane < 64
    ptscale = jnp.where(lane < 64, 1.0, -1.0) * ((lane % 64) // 16 + 1).astype(F32)

    def packed_rows(si, low, high):
        slot, half = ((0, 0), (0, 1), (1, 0), (1, 1), (2, 0), (3, 0), (3, 1), (4, 0), (4, 1))[si]
        part = slice(low, high)
        right, grp, plc = fright[part], fgroup[part], fplace[part]
        x, z = col_r[slot, part, :].astype(F32), col_l[slot, part, :].astype(F32)
        merged = jnp.where(right, roll(x, 64) if half else x, z if half else roll(z, 64))
        for g in range(HALF):
            a = ext[si * ANG + HALF - g - 1, part, 0:LANES].astype(F32)
            b = ext[si * ANG + HALF + g + 1, part, cols - LANES : cols].astype(F32)
            merged = jnp.where(right & (grp == g) & (plc < 2), roll(b, 16 * g + 2), merged)
            merged = jnp.where((~right) & (grp == g) & (plc >= 14), roll(a, 16 * g + 78), merged)
        pb[si, part, :] = merged

    def packed_step(si, low, high):
        s = si - HALF
        base, size = PAD + D0 * s + low, high - low
        v0 = pb[si, base : base + size, :]
        side = ptscale[low:high] * (roll(v0, -1) - roll(v0, 1))
        data, src = terms(v0, side, difference(pb, (si,), base, size, s) if s else None, s, cpack[low:high, :])
        pacc[0, low:high, :] += data
        pacc[1, low:high, :] += src

    for si in range(ANG):
        packed_rows(si, PAD, PAD + rows)
        packed_step(si, *inner_rows(si - HALF))
    learn(4)

    def combine(low, high):
        part = slice(low, high)
        place_of = lane_of(high - low)
        for f in range(2):
            ta, tb = acc[HALF, f, 0, part, :], acc[HALF, f, 1, part, :]
            strip = pacc[f, part, :]
            for ti in range(ANG):
                m = D0 * abs(ti - HALF)
                if m == 0:
                    continue
                a, b = acc[ti, f, 0, part, :], acc[ti, f, 1, part, :]
                g = m // D0 - 1
                if ti > HALF:
                    ra, rb = roll(a, -m), roll(b, -m)
                    ta = ta + jnp.where(place_of < LANES - m, ra, rb)
                    tb = tb + jnp.where(place_of <= LANES - 2 - m, rb, roll(strip, 126 - m - 16 * g))
                else:
                    ra, rb = roll(a, m), roll(b, m)
                    ta = ta + jnp.where(place_of >= m + 1, ra, roll(strip, m - 78 - 16 * g))
                    tb = tb + jnp.where(place_of >= m, rb, ra)
            own[f, part, 0:LANES] = ta
            own[f, part, LANES : 2 * LANES] = tb

    def edge_sizes(sizes):
        for ti in range(ANG):
            spans = []
            for size in sizes:
                spans.append((view_of(ti, size), PAD + rows, PAD + rows + PAD))
                spans.append((view_of(ti, -size), 0, PAD))
            widen(ti, spans)
            for at in (0, chunk, rows - 2 * chunk, rows - chunk):
                sums = [[acc[ti, f, h, at : at + chunk, :] for h in range(2)] for f in range(2)]
                middle = [cen[ti, h, at : at + chunk, :] for h in range(2)]
                for size in sizes:
                    s = -size if at < rows // 2 else size
                    low, high = inner_rows(s)
                    if not low <= at < high:
                        view_step(view_of(ti, s), s, at, middle, sums)
                for f in range(2):
                    for h in range(2):
                        acc[ti, f, h, at : at + chunk, :] = sums[f][h]
        for size in sizes:
            for s in (-size, size):
                first = 0 if s < 0 else PAD + rows
                packed_rows(HALF + s, first, first + PAD)
                low, high = inner_rows(s)
                packed_step(HALF + s, *((0, low) if s < 0 else (high, rows)))

    combine(PAD, rows - PAD)
    for sizes in GROUPS:
        for size in sizes:
            arrive(row_copies[2 * size : 2 * size + 2])
        edge_sizes(sizes)
    combine(0, PAD)
    combine(rows - PAD, rows)

    coeff = damping + own[0] * (0.25 / VIEWS)
    source = own[1] * (-0.5 / VIEWS)

    inner = (slice(8, 8 + rows), slice(LANES, LANES + cols))
    zed = source / (coeff + weights[inner])
    zc[0] = zed
    zc[1] = coeff
    gpack[0] = jnp.where(right_part, zed[:, 0:LANES], roll(coeff[:, 0:LANES], 64))
    gpack[1] = jnp.where(right_part, roll(coeff[:, cols - LANES : cols], 64), zed[:, cols - LANES : cols])

    copies2 = []
    for index, (dr, dc) in enumerate(DIRS):
        if dc == 0:
            src = zc.at[:, pl.ds(0, 8), :] if dr < 0 else zc.at[:, pl.ds(rows - 8, 8), :]
            dst = ghost_d if dr < 0 else ghost_u
        elif dr == 0:
            src = gpack.at[0] if dc < 0 else gpack.at[1]
            dst = ghost_r if dc < 0 else ghost_l
        else:
            src = gpack.at[0 if dc < 0 else 1, pl.ds(0 if dr < 0 else rows - 8, 8), :]
            dst = corner.at[index - 4]
        copies2.append((dr, dc, pltpu.make_async_remote_copy(
            src_ref=src, dst_ref=dst, send_sem=send2.at[index], recv_sem=recv2.at[index],
            device_id=(r + dr, c + dc), device_id_type=pl.DeviceIdType.MESH)))
    start(copies2)
    drain(row_copies + col_copies)
    for step in range(5, len(reaches) + 1):
        learn(step)
    arrive(copies2)

    zf = jnp.concatenate([
        jnp.concatenate([corner[3], ghost_u[0], corner[2]], axis=1),
        jnp.concatenate([ghost_l[...], zed, ghost_r[...]], axis=1),
        jnp.concatenate([corner[1], ghost_d[0], corner[0]], axis=1)], axis=0)
    one = jnp.ones((8, LANES), F32)
    kf = jnp.concatenate([
        jnp.concatenate([one, ghost_u[1], one], axis=1),
        jnp.concatenate([roll(ghost_l[...], 64), coeff, roll(ghost_r[...], 64)], axis=1),
        jnp.concatenate([one, ghost_d[1], one], axis=1)], axis=0)
    diag = kf + weights

    def gather(z):
        return edge_e * east(z) + edge_w * west(z) + edge_s * south(z) + edge_n * north(z)

    around = gather(zf)
    yf = around / diag
    n1, y = around[inner], yf[inner]
    n2 = gather(yf)[inner]
    w = source - n1
    q = zed - y
    wv = n1 - n2
    v = w - wv
    sums = (y * n1, q * n1, q * w, y * wv, y * v, q * v)
    line = lax.broadcasted_iota(jnp.int32, (1, LANES), 1)
    packed = jnp.zeros((1, LANES), F32)
    for i, x in enumerate(sums):
        x = jnp.sum(x, axis=0, keepdims=True)
        x = jnp.sum(x, axis=1, keepdims=True)
        packed = jnp.where(line == i, x, packed)
    redout[0] = packed
    redbuf[me] = packed

    def red_copy(i):
        peer = (me + i) % count
        return pltpu.make_async_remote_copy(
            src_ref=redout.at[0], dst_ref=redbuf.at[me], send_sem=rsend.at[0], recv_sem=rrecv.at[0],
            device_id=(peer // ncol, peer % ncol), device_id_type=pl.DeviceIdType.MESH)

    def cast_out(i, carry):
        red_copy(i).start()
        return carry

    lax.fori_loop(1, count, cast_out, 0)
    drain(copies2)
    others = redbuf.at[pl.ds(0, count - 1)]
    pltpu.make_async_copy(others, others, rrecv.at[0]).wait()
    pltpu.make_async_copy(others, others, rsend.at[0]).wait()
    totals = jnp.sum(redbuf[...], axis=0)
    f, g, h, k, l, m = [totals[:, i : i + 1] for i in range(6)]
    b, e = g + h, f + g
    delta = e / b
    step0 = (e + b) / b
    rz0 = e + b
    rz1 = f - 2.0 * delta * g + delta * delta * h
    wu1 = k - 2.0 * delta * l + delta * delta * m
    beta = rz1 / rz0
    step1 = rz1 / (wu1 - beta * rz1 / step0)
    direction = (y - delta * q) + beta * zed
    image = (wv - delta * v) + beta * w
    out[0] = step0 * zed + step1 * direction
    out[1] = (n1 - delta * w) - step1 * image


def solution(mesh):
    nrow, ncol = mesh.shape["row"], mesh.shape["col"]

    def shards(views):
        _, rows, cols = views.shape
        full = PAD + rows + PAD
        bf = views.dtype
        out = pl.pallas_call(
            functools.partial(kernel, nrow, ncol),
            out_shape=jax.ShapeDtypeStruct((2, rows, cols), F32),
            in_specs=[pl.BlockSpec(memory_space=pltpu.HBM)],
            out_specs=pl.BlockSpec(memory_space=pltpu.VMEM),
            scratch_shapes=[
                pltpu.VMEM((VIEWS, full, cols), bf),
                pltpu.VMEM((2, 5, rows, LANES), bf),
                pltpu.VMEM((5, full, LANES), bf),
                pltpu.VMEM((5, full, LANES), bf),
                pltpu.VMEM((VIEWS, 2, full, LANES), F32),
                pltpu.VMEM((VIEWS, 2, full, LANES), F32),
                pltpu.VMEM((ANG, cols, cols), bf),
                pltpu.VMEM((ANG, full, LANES), F32),
                pltpu.VMEM((ANG, 2, rows, LANES), F32),
                pltpu.VMEM((rows, LANES), F32),
                pltpu.VMEM((ANG, 2, 2, rows, LANES), F32),
                pltpu.VMEM((2, rows, LANES), F32),
                pltpu.VMEM((2, rows, cols), F32),
                pltpu.VMEM((2, rows, cols), F32),
                pltpu.VMEM((2, rows, LANES), F32),
                pltpu.VMEM((2, 8, cols), F32),
                pltpu.VMEM((2, 8, cols), F32),
                pltpu.VMEM((rows, LANES), F32),
                pltpu.VMEM((rows, LANES), F32),
                pltpu.VMEM((4, 8, LANES), F32),
                pltpu.VMEM((nrow * ncol, 1, LANES), F32),
                pltpu.VMEM((1, 1, LANES), F32),
                pltpu.SemaphoreType.DMA((ANG,)),
                pltpu.SemaphoreType.DMA((16,)),
                pltpu.SemaphoreType.DMA((16,)),
                pltpu.SemaphoreType.DMA((8,)),
                pltpu.SemaphoreType.DMA((8,)),
                pltpu.SemaphoreType.DMA((1,)),
                pltpu.SemaphoreType.DMA((1,)),
                pltpu.SemaphoreType.REGULAR((8,)),
            ],
            compiler_params=pltpu.CompilerParams(collective_id=0, has_side_effects=True, vmem_limit_bytes=48 << 20),
        )(pltpu.with_memory_space_constraint(views, pltpu.HBM))
        return out[0], out[1]

    return jax.shard_map(
        shards,
        mesh=mesh,
        in_specs=(P(None, "row", "col"),),
        out_specs=(P("row", "col"), P("row", "col")),
        check_vma=False,
    )
```

```python
import functools

import jax
import jax.numpy as jnp
from jax import lax
from jax.experimental import pallas as pl
from jax.experimental.pallas import tpu as pltpu
from jax.sharding import PartitionSpec as P

ANG = 9
VIEWS = 81
HALF = 4
CENTER = 40
D0 = 3
smooth_weight = 2.0
damping = 0.1
PAD = 16
RING = 8
GROUPS = ((0, 1, 2, 3), (4,))
STRIP = (50, 42, 31, 17, 0)
LANES = 128
F32 = jnp.float32
DIRS = ((-1, 0), (1, 0), (0, -1), (0, 1), (-1, -1), (-1, 1), (1, -1), (1, 1))


def roll(x, shift):
    return pltpu.roll(x, shift % LANES, 1)


def lane_of(rows):
    return lax.broadcasted_iota(jnp.int32, (rows, LANES), 1)


def kernel(nrow, ncol, views, out, ext, sp, col_r, col_l, side_r, side_l, fb, sb, band, pb, cen, cpack, acc, pacc, own,
           redbuf, redout, load_sem, send1, recv1, rsend, rrecv, known):
    rows, cols = views.shape[1], views.shape[2]
    r, c = lax.axis_index("row"), lax.axis_index("col")
    count = nrow * ncol
    me = r * ncol + c
    full = PAD + rows + PAD

    def exists(dr, dc):
        return (r + dr >= 0) & (r + dr < nrow) & (c + dc >= 0) & (c + dc < ncol)

    barrier = pltpu.get_barrier_semaphore()

    def greet(sem, far, dirs):
        for dr, dc in dirs:
            if abs(dr) * far < nrow and abs(dc) * far < ncol:
                @pl.when(exists(dr * far, dc * far))
                def _():
                    pl.semaphore_signal(sem, inc=1, device_id=(r + dr * far, c + dc * far), device_id_type=pl.DeviceIdType.MESH)

    def met(sem, far, dirs):
        total = 0
        for dr, dc in dirs:
            if abs(dr) * far < nrow and abs(dc) * far < ncol:
                total = total + jnp.where(exists(dr * far, dc * far), 1, 0)
        pl.semaphore_wait(sem, total)

    greet(barrier, 1, DIRS[:4])
    rounds = [(1, DIRS[:4])]
    while len(rounds) == 1 or 2 * rounds[-1][0] < max(nrow, ncol) - 1:
        rounds.append((1 << (len(rounds) - 1), DIRS))

    def learn(step):
        if 0 < step <= len(rounds):
            met(known.at[step - 1], *rounds[step - 1])
        if step < len(rounds):
            greet(known.at[step], *rounds[step])

    loads = []
    for si in range(ANG):
        part = pl.ds(si * ANG, ANG)
        copy = pltpu.make_async_copy(views.at[part], ext.at[part, pl.ds(PAD, rows), :], load_sem.at[si])
        copy.start()
        loads.append(copy)

    def zero(ref, first, number, row, size):
        def body(i, carry):
            ref[first + i, row : row + size, :] = jnp.zeros((size, ref.shape[2]), ref.dtype)
            return carry
        lax.fori_loop(0, number, body, 0)

    @pl.when(r == 0)
    def _():
        zero(ext, 0, 41, 0, PAD)

    @pl.when(r == nrow - 1)
    def _():
        zero(ext, 40, 41, PAD + rows, PAD)

    for ref, edge in ((col_r, c == ncol - 1), (col_l, c == 0)):
        @pl.when(edge)
        def _():
            zero(ref, 0, 5, PAD, rows)

        @pl.when(edge | (r == 0))
        def _():
            zero(ref, 0, 3, 0, PAD)

        @pl.when(edge | (r == nrow - 1))
        def _():
            zero(ref, 2, 3, PAD + rows, PAD)

    row_copies = []
    for size in range(HALF + 1):
        reach = 8 if D0 * size + 3 <= 8 else PAD
        for index, (dr, dc) in enumerate(DIRS[:2]):
            if size == 0:
                part = pl.ds(ANG * HALF, ANG)
            else:
                part = pl.ds(ANG * (HALF - dr * size), ANG)
            if dr < 0:
                src, dst = views.at[part, pl.ds(0, reach), :], ext.at[part, pl.ds(PAD + rows, reach), :]
            else:
                src, dst = views.at[part, pl.ds(rows - reach, reach), :], ext.at[part, pl.ds(PAD - reach, reach), :]
            row_copies.append((dr, dc, pltpu.make_async_remote_copy(
                src_ref=src, dst_ref=dst, send_sem=send1.at[2 * size + index], recv_sem=recv1.at[2 * size + index],
                device_id=(r + dr, c + dc), device_id_type=pl.DeviceIdType.MESH)))
    col_copies = []
    for index, (dr, dc) in enumerate(DIRS[2:]):
        side = col_r if dc < 0 else col_l
        mine = sp.at[0 if dc < 0 else 1]
        if dr == 0:
            src, dst = mine, side.at[:, pl.ds(PAD, rows), :]
        elif dr < 0:
            src, dst = mine.at[pl.ds(2, 3), pl.ds(0, PAD), :], side.at[pl.ds(2, 3), pl.ds(PAD + rows, PAD), :]
        else:
            src, dst = mine.at[pl.ds(0, 3), pl.ds(rows - PAD, PAD), :], side.at[pl.ds(0, 3), pl.ds(0, PAD), :]
        col_copies.append((dr, dc, pltpu.make_async_remote_copy(
            src_ref=src, dst_ref=dst, send_sem=send1.at[10 + index], recv_sem=recv1.at[10 + index],
            device_id=(r + dr, c + dc), device_id_type=pl.DeviceIdType.MESH)))

    side_copies = []
    for index, (dr, dc) in enumerate(DIRS[2:]):
        side = side_r if dc < 0 else side_l
        tile = pl.ds(0 if dc < 0 else cols - LANES, LANES)
        first, number, into = ((0, rows, PAD), (rows - RING, RING, PAD - RING), (0, RING, PAD + rows))[dr]
        side_copies.append((dr, dc, pltpu.make_async_remote_copy(
            src_ref=views.at[CENTER, pl.ds(first, number), tile], dst_ref=side.at[pl.ds(into, number), :],
            send_sem=send1.at[16 + index], recv_sem=recv1.at[16 + index],
            device_id=(r + dr, c + dc), device_id_type=pl.DeviceIdType.MESH)))

    def start(group):
        for dr, dc, copy in group:
            @pl.when(exists(dr, dc))
            def _():
                copy.start()

    def arrive(group):
        for dr, dc, copy in group:
            @pl.when(exists(-dr, -dc))
            def _():
                copy.wait_recv()

    def drain(group):
        for dr, dc, copy in group:
            @pl.when(exists(dr, dc))
            def _():
                copy.wait_send()

    offset = lax.broadcasted_iota(jnp.int32, (cols, cols), 0) - lax.broadcasted_iota(jnp.int32, (cols, cols), 1)
    plain = jnp.where(offset == 1, 1.0, jnp.where(offset == -1, -1.0, 0.0))
    for ti in range(ANG):
        band[ti] = (plain * float(ti - HALF)).astype(band.dtype)

    met(barrier, 1, DIRS[:4])
    start(row_copies)
    start(side_copies[:2])
    learn(0)
    for copy in loads:
        copy.wait()

    lane = lane_of(rows)
    right_part = lane < 64

    def own_start(t):
        return STRIP[t] + (2 if t else 1)

    for slot, pair in enumerate(((0, 1), (2, 3), (4,), (5, 6), (7, 8))):
        left = right = None
        for half, si in enumerate(pair):
            for t in range(HALF, -1, -1):
                first = own_start(t) + 64 * half
                x = roll(ext[si * ANG + HALF + t, PAD : PAD + rows, 0:LANES].astype(F32), first)
                left = x if left is None else jnp.where(lane >= first, x, left)
        for half, si in reversed(list(enumerate(pair))):
            for t in range(HALF, -1, -1):
                first = STRIP[t] + 64 * (1 - half)
                x = roll(ext[si * ANG + HALF - t, PAD : PAD + rows, cols - LANES : cols].astype(F32), first - (LANES - 3 - D0 * t))
                right = x if right is None else jnp.where(lane >= first, x, right)
        sp[0, slot] = left.astype(sp.dtype)
        sp[1, slot] = right.astype(sp.dtype)
    start(col_copies[:2])
    learn(1)
    start(side_copies[2:] + col_copies[2:])
    arrive(side_copies[:2])

    def build_center(low, high):
        part, into = slice(PAD + low, PAD + high), slice(RING + low, RING + high)
        at = lane_of(high - low)
        tl, tr = side_l[part, :].astype(F32), side_r[part, :].astype(F32)
        ta, tb = [ext[CENTER, part, h * LANES : (h + 1) * LANES].astype(F32) for h in range(2)]
        for ti in range(ANG):
            move = D0 * (ti - HALF)
            if move > 0:
                ra = roll(ta, move)
                cen[ti, 0, into, :] = jnp.where(at >= move, ra, roll(tl, move))
                cen[ti, 1, into, :] = jnp.where(at >= move, roll(tb, move), ra)
            elif move < 0:
                rb = roll(tb, move)
                cen[ti, 0, into, :] = jnp.where(at < LANES + move, roll(ta, move), rb)
                cen[ti, 1, into, :] = jnp.where(at < LANES + move, rb, roll(tr, move))
            else:
                cen[ti, 0, into, :] = ta
                cen[ti, 1, into, :] = tb
        total = None
        for t in range(HALF, -1, -1):
            m = D0 * t
            first = STRIP[t]
            inside = own_start(t) + m
            x = jnp.where(at >= inside, roll(tr, inside), roll(tb, inside))
            total = x if total is None else jnp.where(at >= first, x, total)
        for t in range(HALF, -1, -1):
            first = 64 + STRIP[t]
            x = jnp.where(at >= first + 3, roll(ta, first + 3), roll(tl, first + 3))
            total = jnp.where(at >= first, x, total)
        cpack[into, :] = total

    build_center(0, rows)
    pacc[...] = jnp.zeros_like(pacc)

    chunk = 8

    def terms(v0, side, down, s, middle):
        if s == 0:
            slope = side
        else:
            slope = side + (down if abs(s) == 1 else float(abs(s)) * down)
        error = v0 - middle
        weighted = slope * lax.rsqrt(1.0 + error * error)
        return weighted * slope, weighted * error

    def difference(ref, head, base, size, s):
        after, before = (base + 1, base - 1) if s > 0 else (base - 1, base + 1)
        return ref[head + (slice(after, after + size), slice(None))] - ref[head + (slice(before, before + size), slice(None))]

    def view_step(k, s, at, middle, sums):
        base = RING + PAD + D0 * s + at
        for h in range(2):
            v0, side = fb[k, h, base : base + chunk, :], sb[k, h, base : base + chunk, :]
            data, src = terms(v0, side, difference(fb, (k, h), base, chunk, s) if s else None, s, middle[h])
            sums[0][h] = data if sums[0][h] is None else sums[0][h] + data
            sums[1][h] = src if sums[1][h] is None else sums[1][h] + src

    def widen(ti, spans):
        part = jnp.concatenate([ext[k, low:high, :] for k, low, high in spans], axis=0)
        wide = part.astype(F32)
        side = jnp.dot(part, band[ti], preferred_element_type=F32)
        first = 0
        for k, low, high in spans:
            rest = slice(first, first + high - low)
            for h in range(2):
                fb[k, h, RING + low : RING + high, :] = wide[rest, h * LANES : (h + 1) * LANES]
                sb[k, h, RING + low : RING + high, :] = side[rest, h * LANES : (h + 1) * LANES]
            first += high - low

    def view_of(ti, s):
        return ANG * (s + HALF) + ti

    def inner_rows(s):
        reach = -(-(D0 * abs(s) + 1) // chunk) * chunk if s else 0
        return (reach if s < 0 else 0), (rows - reach if s > 0 else rows)

    def inner_pass(ti):
        for s in range(-HALF, HALF + 1):
            widen(ti, [(view_of(ti, s), PAD, PAD + rows)])
        for at in range(0, rows, chunk):
            sums = [[None, None], [None, None]]
            middle = [cen[ti, h, RING + at : RING + at + chunk, :] for h in range(2)]
            for s in range(-HALF, HALF + 1):
                low, high = inner_rows(s)
                if low <= at < high:
                    view_step(view_of(ti, s), s, at, middle, sums)
            for f in range(2):
                for h in range(2):
                    acc[ti, f, h, RING + at : RING + at + chunk, :] = sums[f][h]

    for ti in range(ANG):
        inner_pass(ti)
        if ti % 3 == 2:
            learn(ti // 3 + 2)
    arrive(row_copies[:2] + col_copies + side_copies[2:])
    build_center(-RING, 0)
    build_center(rows, rows + RING)
    frows, fcols = rows + 16, cols + 2 * LANES
    middle_rows = slice(PAD - RING, PAD + rows + RING)
    cf = jnp.concatenate([
        side_l[0:full, :].astype(F32), ext[CENTER, 0:full, :].astype(F32), side_r[0:full, :].astype(F32)], axis=1)[middle_rows]
    gcol = lax.broadcasted_iota(jnp.int32, (frows, fcols), 1) + (c * cols - LANES)
    grow = lax.broadcasted_iota(jnp.int32, (frows, fcols), 0) + (r * rows - 8)

    def east(x):
        return pltpu.roll(x, fcols - 1, 1)

    def west(x):
        return pltpu.roll(x, 1, 1)

    def south(x):
        return pltpu.roll(x, frows - 1, 0)

    def north(x):
        return pltpu.roll(x, 1, 0)

    dx = east(cf) - cf
    dy = south(cf) - cf
    edge_e = jnp.where((gcol >= 0) & (gcol < ncol * cols - 1), smooth_weight * jnp.exp(-dx * dx), 0.0)
    edge_s = jnp.where((grow >= 0) & (grow < nrow * rows - 1), smooth_weight * jnp.exp(-dy * dy), 0.0)
    edge_w, edge_n = west(edge_e), north(edge_s)
    weights = edge_e + edge_w + edge_s + edge_n

    def packed_rows(si, low, high):
        slot, half = ((0, 0), (0, 1), (1, 0), (1, 1), (2, 0), (3, 0), (3, 1), (4, 0), (4, 1))[si]
        at = lane_of(high - low)
        part = slice(low, high)
        x, z = col_r[slot, part, :].astype(F32), col_l[slot, part, :].astype(F32)
        merged = roll(jnp.where(at < 64, z, x), 64) if half else jnp.where(at < 64, x, z)
        for t in range(HALF + 1):
            a = ext[si * ANG + HALF - t, part, 0:LANES].astype(F32)
            b = ext[si * ANG + HALF + t, part, cols - LANES : cols].astype(F32)
            first, last = STRIP[t], own_start(t) - 1
            own_b = (at >= first) & (at <= last) if t else at == first
            merged = jnp.where(own_b, roll(b, last - (LANES - 1)), merged)
            first = 64 + STRIP[t] + 3 + D0 * t
            own_a = (at == first) | (at == first + 1) if t else at == first
            merged = jnp.where(own_a, roll(a, first), merged)
        pb[si, RING + low : RING + high, :] = merged

    def packed_step(si, low, high):
        s = si - HALF
        base, size = RING + PAD + D0 * s + low, high - low
        at = lane_of(size)
        scale = jnp.zeros((size, LANES), F32)
        for t in range(1, HALF + 1):
            span = 5 + D0 * t
            scale = jnp.where((at >= STRIP[t]) & (at < STRIP[t] + span), float(t), scale)
            scale = jnp.where((at >= 64 + STRIP[t]) & (at < 64 + STRIP[t] + span), float(-t), scale)
        v0 = pb[si, base : base + size, :]
        side = scale * (roll(v0, -1) - roll(v0, 1))
        part = slice(RING + low, RING + high)
        data, src = terms(v0, side, difference(pb, (si,), base, size, s) if s else None, s, cpack[part, :])
        pacc[0, part, :] += data
        pacc[1, part, :] += src

    for si in range(ANG):
        packed_rows(si, PAD, PAD + rows)
        packed_step(si, *inner_rows(si - HALF))
    learn(5)

    def combine(low, high):
        part = slice(RING + low, RING + high)
        at = lane_of(high - low)
        for f in range(2):
            ta, tb = acc[HALF, f, 0, part, :], acc[HALF, f, 1, part, :]
            strip = pacc[f, part, :]
            el, er = roll(strip, 61 - STRIP[0]), roll(strip, -own_start(0))
            for ti in range(ANG):
                m = D0 * abs(ti - HALF)
                if m == 0:
                    continue
                a, b = acc[ti, f, 0, part, :], acc[ti, f, 1, part, :]
                t = m // D0
                if ti > HALF:
                    ra, rb, rs = roll(a, -m), roll(b, -m), roll(strip, 126 - m - STRIP[t])
                    ta = ta + jnp.where(at < LANES - m, ra, rb)
                    tb = tb + jnp.where(at <= LANES - 2 - m, rb, rs)
                    el, er = el + ra, er + rs
                else:
                    ra, rb, rs = roll(a, m), roll(b, m), roll(strip, -67 - STRIP[t])
                    ta = ta + jnp.where(at >= m + 1, ra, rs)
                    tb = tb + jnp.where(at >= m, rb, ra)
                    el, er = el + rs, er + rb
            for tile, total in enumerate((el, ta, tb, er)):
                own[f, part, tile * LANES : (tile + 1) * LANES] = total

    def edge_sizes(sizes):
        for ti in range(ANG):
            spans = []
            for size in sizes:
                spans.append((view_of(ti, size), PAD + rows, PAD + rows + PAD))
                spans.append((view_of(ti, -size), 0, PAD))
            widen(ti, spans)
            for at in (-RING, 0, chunk, rows - 2 * chunk, rows - chunk, rows):
                ring = at < 0 or at >= rows
                part = slice(RING + at, RING + at + chunk)
                if ring and sizes == GROUPS[0]:
                    sums = [[None, None], [None, None]]
                else:
                    sums = [[acc[ti, f, h, part, :] for h in range(2)] for f in range(2)]
                middle = [cen[ti, h, part, :] for h in range(2)]
                for size in sizes:
                    for s in ((-size, size) if size else (0,)):
                        low, high = inner_rows(s)
                        if not low <= at < high:
                            view_step(view_of(ti, s), s, at, middle, sums)
                for f in range(2):
                    for h in range(2):
                        acc[ti, f, h, part, :] = sums[f][h]
        for size in sizes:
            if size == 0:
                packed_rows(HALF, 0, PAD)
                packed_rows(HALF, PAD + rows, full)
            else:
                packed_rows(HALF - size, 0, PAD)
                packed_rows(HALF + size, PAD + rows, full)
            for s in ((-size, size) if size else (0,)):
                low, high = inner_rows(s)
                packed_step(HALF + s, -RING, low)
                packed_step(HALF + s, high, rows + RING)

    combine(PAD, rows - PAD)
    for sizes in GROUPS:
        for size in sizes:
            if size:
                arrive(row_copies[2 * size : 2 * size + 2])
        edge_sizes(sizes)
    combine(-RING, PAD)
    combine(rows - PAD, rows + RING)

    inside = (gcol >= 0) & (gcol < ncol * cols) & (grow >= 0) & (grow < nrow * rows)
    coeff = damping + own[0] * (0.25 / VIEWS)
    field = own[1] * (-0.5 / VIEWS)
    diag = jnp.where(inside, coeff + weights, 1.0)
    zf = jnp.where(inside, field / diag, 0.0)
    inner = (slice(RING, RING + rows), slice(LANES, LANES + cols))
    source, zed = field[inner], zf[inner]

    def gather(z):
        return edge_e * east(z) + edge_w * west(z) + edge_s * south(z) + edge_n * north(z)

    around = gather(zf)
    yf = around / diag
    n1, y = around[inner], yf[inner]
    n2 = gather(yf)[inner]
    w = source - n1
    q = zed - y
    wv = n1 - n2
    v = w - wv
    sums = (y * n1, q * n1, q * w, y * wv, y * v, q * v)
    line = lax.broadcasted_iota(jnp.int32, (1, LANES), 1)
    packed = jnp.zeros((1, LANES), F32)
    for i, x in enumerate(sums):
        x = jnp.sum(x, axis=0, keepdims=True)
        x = jnp.sum(x, axis=1, keepdims=True)
        packed = jnp.where(line == i, x, packed)
    for step in range(6, len(rounds) + 1):
        learn(step)
    redout[0] = packed
    redbuf[me] = packed

    def red_copy(i):
        peer = (me + i) % count
        return pltpu.make_async_remote_copy(
            src_ref=redout.at[0], dst_ref=redbuf.at[me], send_sem=rsend.at[0], recv_sem=rrecv.at[0],
            device_id=(peer // ncol, peer % ncol), device_id_type=pl.DeviceIdType.MESH)

    def cast_out(i, carry):
        red_copy(i).start()
        return carry

    lax.fori_loop(1, count, cast_out, 0)
    drain(row_copies + side_copies + col_copies)
    others = redbuf.at[pl.ds(0, count - 1)]
    pltpu.make_async_copy(others, others, rrecv.at[0]).wait()
    pltpu.make_async_copy(others, others, rsend.at[0]).wait()
    totals = jnp.sum(redbuf[...], axis=0)
    f, g, h, k, l, m = [totals[:, i : i + 1] for i in range(6)]
    b, e = g + h, f + g
    delta = e / b
    step0 = (e + b) / b
    rz0 = e + b
    rz1 = f - 2.0 * delta * g + delta * delta * h
    wu1 = k - 2.0 * delta * l + delta * delta * m
    beta = rz1 / rz0
    step1 = rz1 / (wu1 - beta * rz1 / step0)
    direction = (y - delta * q) + beta * zed
    image = (wv - delta * v) + beta * w
    out[0] = step0 * zed + step1 * direction
    out[1] = (n1 - delta * w) - step1 * image


def solution(mesh):
    nrow, ncol = mesh.shape["row"], mesh.shape["col"]

    def shards(views):
        _, rows, cols = views.shape
        full = PAD + rows + PAD
        bf = views.dtype
        out = pl.pallas_call(
            functools.partial(kernel, nrow, ncol),
            out_shape=jax.ShapeDtypeStruct((2, rows, cols), F32),
            in_specs=[pl.BlockSpec(memory_space=pltpu.HBM)],
            out_specs=pl.BlockSpec(memory_space=pltpu.VMEM),
            scratch_shapes=[
                pltpu.VMEM((VIEWS, full, cols), bf),
                pltpu.VMEM((2, 5, rows, LANES), bf),
                pltpu.VMEM((5, full, LANES), bf),
                pltpu.VMEM((5, full, LANES), bf),
                pltpu.VMEM((full, LANES), bf),
                pltpu.VMEM((full, LANES), bf),
                pltpu.VMEM((VIEWS, 2, full + 2 * RING, LANES), F32),
                pltpu.VMEM((VIEWS, 2, full + 2 * RING, LANES), F32),
                pltpu.VMEM((ANG, cols, cols), bf),
                pltpu.VMEM((ANG, full + 2 * RING, LANES), F32),
                pltpu.VMEM((ANG, 2, rows + 2 * RING, LANES), F32),
                pltpu.VMEM((rows + 2 * RING, LANES), F32),
                pltpu.VMEM((ANG, 2, 2, rows + 2 * RING, LANES), F32),
                pltpu.VMEM((2, rows + 2 * RING, LANES), F32),
                pltpu.VMEM((2, rows + 2 * RING, cols + 2 * LANES), F32),
                pltpu.VMEM((nrow * ncol, 1, LANES), F32),
                pltpu.VMEM((1, 1, LANES), F32),
                pltpu.SemaphoreType.DMA((ANG,)),
                pltpu.SemaphoreType.DMA((22,)),
                pltpu.SemaphoreType.DMA((22,)),
                pltpu.SemaphoreType.DMA((1,)),
                pltpu.SemaphoreType.DMA((1,)),
                pltpu.SemaphoreType.REGULAR((8,)),
            ],
            compiler_params=pltpu.CompilerParams(collective_id=0, has_side_effects=True, vmem_limit_bytes=48 << 20),
        )(pltpu.with_memory_space_constraint(views, pltpu.HBM))
        return out[0], out[1]

    return jax.shard_map(
        shards,
        mesh=mesh,
        in_specs=(P(None, "row", "col"),),
        out_specs=(P("row", "col"), P("row", "col")),
        check_vma=False,
    )
```

```python
import functools

import jax
import jax.numpy as jnp
from jax import lax
from jax.experimental import pallas as pl
from jax.experimental.pallas import tpu as pltpu
from jax.sharding import PartitionSpec as P

ANG = 9
VIEWS = 81
HALF = 4
CENTER = 40
D0 = 3
smooth_weight = 2.0
damping = 0.1
PAD = 16
RING = 8
GROUPS = ((0, 1, 2, 3), (4,))
STRIP = (50, 42, 31, 17, 0)
LANES = 128
F32 = jnp.float32
DIRS = ((-1, 0), (1, 0), (0, -1), (0, 1), (-1, -1), (-1, 1), (1, -1), (1, 1))


def roll(x, shift):
    return pltpu.roll(x, shift % LANES, 1)


def lane_of(rows):
    return lax.broadcasted_iota(jnp.int32, (rows, LANES), 1)


def kernel(nrow, ncol, views, out, ext, sp, col_r, col_l, side_r, side_l, fb, sb, band, pb, cen, cpack, acc, pacc, own,
           redbuf, redout, load_sem, send1, recv1, rsend, rrecv, known):
    rows, cols = views.shape[1], views.shape[2]
    r, c = lax.axis_index("row"), lax.axis_index("col")
    count = nrow * ncol
    me = r * ncol + c
    full = PAD + rows + PAD

    def exists(dr, dc):
        return (r + dr >= 0) & (r + dr < nrow) & (c + dc >= 0) & (c + dc < ncol)

    barrier = pltpu.get_barrier_semaphore()

    def greet(sem, far, dirs):
        for dr, dc in dirs:
            if abs(dr) * far < nrow and abs(dc) * far < ncol:
                @pl.when(exists(dr * far, dc * far))
                def _():
                    pl.semaphore_signal(sem, inc=1, device_id=(r + dr * far, c + dc * far), device_id_type=pl.DeviceIdType.MESH)

    def met(sem, far, dirs):
        total = 0
        for dr, dc in dirs:
            if abs(dr) * far < nrow and abs(dc) * far < ncol:
                total = total + jnp.where(exists(dr * far, dc * far), 1, 0)
        pl.semaphore_wait(sem, total)

    greet(barrier, 1, DIRS[:4])
    rounds = []
    while 1 << len(rounds) < nrow + ncol - 2:
        half = (1 << len(rounds)) // 2
        if half:
            steps = [(i, j) for i in range(-2, 3) for j in range(-2, 3) if 0 < abs(i) + abs(j) <= 2]
            rounds.append((half, steps))
        else:
            rounds.append((1, DIRS[:4]))

    def learn(step):
        if 0 < step <= len(rounds):
            met(known.at[step - 1], *rounds[step - 1])
        if step < len(rounds):
            greet(known.at[step], *rounds[step])

    loads = []
    for si in range(ANG):
        part = pl.ds(si * ANG, ANG)
        copy = pltpu.make_async_copy(views.at[part], ext.at[part, pl.ds(PAD, rows), :], load_sem.at[si])
        copy.start()
        loads.append(copy)

    def zero(ref, first, number, row, size):
        def body(i, carry):
            ref[first + i, row : row + size, :] = jnp.zeros((size, ref.shape[2]), ref.dtype)
            return carry
        lax.fori_loop(0, number, body, 0)

    @pl.when(r == 0)
    def _():
        zero(ext, 0, 41, 0, PAD)

    @pl.when(r == nrow - 1)
    def _():
        zero(ext, 40, 41, PAD + rows, PAD)

    for ref, edge in ((col_r, c == ncol - 1), (col_l, c == 0)):
        @pl.when(edge)
        def _():
            zero(ref, 0, 5, PAD, rows)

        @pl.when(edge | (r == 0))
        def _():
            zero(ref, 0, 3, 0, PAD)

        @pl.when(edge | (r == nrow - 1))
        def _():
            zero(ref, 2, 3, PAD + rows, PAD)

    row_copies = []
    for size in range(HALF + 1):
        reach = 8 if D0 * size + 3 <= 8 else PAD
        for index, (dr, dc) in enumerate(DIRS[:2]):
            if size == 0:
                part = pl.ds(ANG * HALF, ANG)
            else:
                part = pl.ds(ANG * (HALF - dr * size), ANG)
            if dr < 0:
                src, dst = views.at[part, pl.ds(0, reach), :], ext.at[part, pl.ds(PAD + rows, reach), :]
            else:
                src, dst = views.at[part, pl.ds(rows - reach, reach), :], ext.at[part, pl.ds(PAD - reach, reach), :]
            row_copies.append((dr, dc, pltpu.make_async_remote_copy(
                src_ref=src, dst_ref=dst, send_sem=send1.at[2 * size + index], recv_sem=recv1.at[2 * size + index],
                device_id=(r + dr, c + dc), device_id_type=pl.DeviceIdType.MESH)))
    col_copies = []
    for index, (dr, dc) in enumerate(DIRS[2:]):
        side = col_r if dc < 0 else col_l
        mine = sp.at[0 if dc < 0 else 1]
        if dr == 0:
            src, dst = mine, side.at[:, pl.ds(PAD, rows), :]
        elif dr < 0:
            src, dst = mine.at[pl.ds(2, 3), pl.ds(0, PAD), :], side.at[pl.ds(2, 3), pl.ds(PAD + rows, PAD), :]
        else:
            src, dst = mine.at[pl.ds(0, 3), pl.ds(rows - PAD, PAD), :], side.at[pl.ds(0, 3), pl.ds(0, PAD), :]
        col_copies.append((dr, dc, pltpu.make_async_remote_copy(
            src_ref=src, dst_ref=dst, send_sem=send1.at[10 + index], recv_sem=recv1.at[10 + index],
            device_id=(r + dr, c + dc), device_id_type=pl.DeviceIdType.MESH)))

    side_copies = []
    for index, (dr, dc) in enumerate(DIRS[2:]):
        side = side_r if dc < 0 else side_l
        tile = pl.ds(0 if dc < 0 else cols - LANES, LANES)
        first, number, into = ((0, rows, PAD), (rows - RING, RING, PAD - RING), (0, RING, PAD + rows))[dr]
        side_copies.append((dr, dc, pltpu.make_async_remote_copy(
            src_ref=views.at[CENTER, pl.ds(first, number), tile], dst_ref=side.at[pl.ds(into, number), :],
            send_sem=send1.at[16 + index], recv_sem=recv1.at[16 + index],
            device_id=(r + dr, c + dc), device_id_type=pl.DeviceIdType.MESH)))

    def start(group):
        for dr, dc, copy in group:
            @pl.when(exists(dr, dc))
            def _():
                copy.start()

    def arrive(group):
        for dr, dc, copy in group:
            @pl.when(exists(-dr, -dc))
            def _():
                copy.wait_recv()

    def drain(group):
        for dr, dc, copy in group:
            @pl.when(exists(dr, dc))
            def _():
                copy.wait_send()

    offset = lax.broadcasted_iota(jnp.int32, (cols, cols), 0) - lax.broadcasted_iota(jnp.int32, (cols, cols), 1)
    plain = jnp.where(offset == 1, 1.0, jnp.where(offset == -1, -1.0, 0.0))
    for ti in range(ANG):
        band[ti] = (plain * float(ti - HALF)).astype(band.dtype)

    met(barrier, 1, DIRS[:4])
    start(row_copies)
    start(side_copies[:2])
    learn(0)

    lane = lane_of(rows)

    def own_start(t):
        return STRIP[t] + (2 if t else 1)

    def narrow_lane(size):
        return lane_of(size).astype(F32).astype(sp.dtype)

    nlane = narrow_lane(rows)
    for slot, pair in enumerate(((0, 1), (2, 3), (4,), (5, 6), (7, 8))):
        left = right = None
        for si in pair:
            loads[si].wait()
        for half, si in enumerate(pair):
            for t in range(HALF, -1, -1):
                first = own_start(t) + 64 * half
                x = roll(ext[si * ANG + HALF + t, PAD : PAD + rows, 0:LANES], first)
                left = x if left is None else jnp.where(nlane >= first, x, left)
        for half, si in reversed(list(enumerate(pair))):
            for t in range(HALF, -1, -1):
                first = STRIP[t] + 64 * (1 - half)
                x = roll(ext[si * ANG + HALF - t, PAD : PAD + rows, cols - LANES : cols], first - (LANES - 3 - D0 * t))
                right = x if right is None else jnp.where(nlane >= first, x, right)
        sp[0, slot] = left
        sp[1, slot] = right
    start(col_copies[:2])
    learn(1)
    start(side_copies[2:] + col_copies[2:])
    arrive(side_copies[:2])

    def build_center(low, high):
        part, into = slice(PAD + low, PAD + high), slice(RING + low, RING + high)
        at = narrow_lane(high - low)
        tl, tr = side_l[part, :], side_r[part, :]
        ta, tb = [ext[CENTER, part, h * LANES : (h + 1) * LANES] for h in range(2)]
        for ti in range(ANG):
            move = D0 * (ti - HALF)
            if move > 0:
                ra = roll(ta, move)
                pair = jnp.where(at >= move, ra, roll(tl, move)), jnp.where(at >= move, roll(tb, move), ra)
            elif move < 0:
                rb = roll(tb, move)
                pair = jnp.where(at < LANES + move, roll(ta, move), rb), jnp.where(at < LANES + move, rb, roll(tr, move))
            else:
                pair = ta, tb
            for h in range(2):
                cen[ti, h, into, :] = pair[h].astype(F32)
        total = None
        for t in range(HALF, -1, -1):
            first = STRIP[t]
            inside = own_start(t) + D0 * t
            x = jnp.where(at >= inside, roll(tr, inside), roll(tb, inside))
            total = x if total is None else jnp.where(at >= first, x, total)
        for t in range(HALF, -1, -1):
            first = 64 + STRIP[t]
            x = jnp.where(at >= first + 3, roll(ta, first + 3), roll(tl, first + 3))
            total = jnp.where(at >= first, x, total)
        cpack[into, :] = total.astype(F32)

    build_center(0, rows)
    pacc[...] = jnp.zeros_like(pacc)

    chunk = 8

    def terms(v0, side, down, s, middle):
        if s == 0:
            slope = side
        else:
            slope = side + (down if abs(s) == 1 else float(abs(s)) * down)
        error = v0 - middle
        weighted = slope * lax.rsqrt(1.0 + error * error)
        return weighted * slope, weighted * error

    def difference(ref, head, base, size, s):
        after, before = (base + 1, base - 1) if s > 0 else (base - 1, base + 1)
        return ref[head + (slice(after, after + size), slice(None))] - ref[head + (slice(before, before + size), slice(None))]

    def view_step(k, s, at, middle, sums):
        base = RING + PAD + D0 * s + at
        for h in range(2):
            v0, side = fb[k, h, base : base + chunk, :], sb[k, h, base : base + chunk, :]
            data, src = terms(v0, side, difference(fb, (k, h), base, chunk, s) if s else None, s, middle[h])
            sums[0][h] = data if sums[0][h] is None else sums[0][h] + data
            sums[1][h] = src if sums[1][h] is None else sums[1][h] + src

    def widen(ti, spans):
        part = jnp.concatenate([ext[k, low:high, :] for k, low, high in spans], axis=0)
        wide = part.astype(F32)
        side = jnp.dot(part, band[ti], preferred_element_type=F32)
        first = 0
        for k, low, high in spans:
            rest = slice(first, first + high - low)
            for h in range(2):
                fb[k, h, RING + low : RING + high, :] = wide[rest, h * LANES : (h + 1) * LANES]
                sb[k, h, RING + low : RING + high, :] = side[rest, h * LANES : (h + 1) * LANES]
            first += high - low

    def view_of(ti, s):
        return ANG * (s + HALF) + ti

    def inner_rows(s):
        reach = -(-(D0 * abs(s) + 1) // chunk) * chunk if s else 0
        return (reach if s < 0 else 0), (rows - reach if s > 0 else rows)

    def inner_pass(ti):
        for s in range(-HALF, HALF + 1):
            widen(ti, [(view_of(ti, s), PAD, PAD + rows)])
        for at in range(0, rows, chunk):
            sums = [[None, None], [None, None]]
            middle = [cen[ti, h, RING + at : RING + at + chunk, :] for h in range(2)]
            for s in range(-HALF, HALF + 1):
                low, high = inner_rows(s)
                if low <= at < high:
                    view_step(view_of(ti, s), s, at, middle, sums)
            for f in range(2):
                for h in range(2):
                    acc[ti, f, h, RING + at : RING + at + chunk, :] = sums[f][h]

    for ti in range(ANG):
        inner_pass(ti)
        if ti in (2, 5):
            learn(ti // 3 + 2)
    arrive(row_copies[:2] + col_copies + side_copies[2:])
    build_center(-RING, 0)
    build_center(rows, rows + RING)
    frows, fcols = rows + 16, cols + 2 * LANES
    middle_rows = slice(PAD - RING, PAD + rows + RING)
    cf = jnp.concatenate([
        side_l[0:full, :].astype(F32), ext[CENTER, 0:full, :].astype(F32), side_r[0:full, :].astype(F32)], axis=1)[middle_rows]
    gcol = lax.broadcasted_iota(jnp.int32, (frows, fcols), 1) + (c * cols - LANES)
    grow = lax.broadcasted_iota(jnp.int32, (frows, fcols), 0) + (r * rows - 8)

    def east(x):
        return pltpu.roll(x, fcols - 1, 1)

    def west(x):
        return pltpu.roll(x, 1, 1)

    def south(x):
        return pltpu.roll(x, frows - 1, 0)

    def north(x):
        return pltpu.roll(x, 1, 0)

    dx = east(cf) - cf
    dy = south(cf) - cf
    edge_e = jnp.where((gcol >= 0) & (gcol < ncol * cols - 1), smooth_weight * jnp.exp(-dx * dx), 0.0)
    edge_s = jnp.where((grow >= 0) & (grow < nrow * rows - 1), smooth_weight * jnp.exp(-dy * dy), 0.0)
    edge_w, edge_n = west(edge_e), north(edge_s)
    weights = edge_e + edge_w + edge_s + edge_n

    def packed_rows(si, low, high):
        slot, half = ((0, 0), (0, 1), (1, 0), (1, 1), (2, 0), (3, 0), (3, 1), (4, 0), (4, 1))[si]
        at = narrow_lane(high - low)
        part = slice(low, high)
        x, z = col_r[slot, part, :], col_l[slot, part, :]
        merged = roll(jnp.where(at < 64, z, x), 64) if half else jnp.where(at < 64, x, z)
        for t in range(HALF + 1):
            a = ext[si * ANG + HALF - t, part, 0:LANES]
            b = ext[si * ANG + HALF + t, part, cols - LANES : cols]
            first, last = STRIP[t], own_start(t) - 1
            own_b = (at >= first) & (at <= last) if t else at == first
            merged = jnp.where(own_b, roll(b, last - (LANES - 1)), merged)
            first = 64 + STRIP[t] + 3 + D0 * t
            own_a = (at >= first) & (at <= first + 1) if t else at == first
            merged = jnp.where(own_a, roll(a, first), merged)
        pb[si, RING + low : RING + high, :] = merged.astype(F32)

    def packed_step(si, low, high):
        s = si - HALF
        base, size = RING + PAD + D0 * s + low, high - low
        at = lane_of(size)
        scale = jnp.zeros((size, LANES), F32)
        for t in range(1, HALF + 1):
            span = 5 + D0 * t
            scale = jnp.where((at >= STRIP[t]) & (at < STRIP[t] + span), float(t), scale)
            scale = jnp.where((at >= 64 + STRIP[t]) & (at < 64 + STRIP[t] + span), float(-t), scale)
        v0 = pb[si, base : base + size, :]
        side = scale * (roll(v0, -1) - roll(v0, 1))
        part = slice(RING + low, RING + high)
        data, src = terms(v0, side, difference(pb, (si,), base, size, s) if s else None, s, cpack[part, :])
        pacc[0, part, :] += data
        pacc[1, part, :] += src

    for si in range(ANG):
        packed_rows(si, PAD, PAD + rows)
        packed_step(si, *inner_rows(si - HALF))
    learn(4)

    def combine(low, high):
        part = slice(RING + low, RING + high)
        at = lane_of(high - low)
        for f in range(2):
            ta, tb = acc[HALF, f, 0, part, :], acc[HALF, f, 1, part, :]
            strip = pacc[f, part, :]
            el, er = roll(strip, 61 - STRIP[0]), roll(strip, -own_start(0))
            for ti in range(ANG):
                m = D0 * abs(ti - HALF)
                if m == 0:
                    continue
                a, b = acc[ti, f, 0, part, :], acc[ti, f, 1, part, :]
                t = m // D0
                if ti > HALF:
                    ra, rb, rs = roll(a, -m), roll(b, -m), roll(strip, 126 - m - STRIP[t])
                    ta = ta + jnp.where(at < LANES - m, ra, rb)
                    tb = tb + jnp.where(at <= LANES - 2 - m, rb, rs)
                    el, er = el + ra, er + rs
                else:
                    ra, rb, rs = roll(a, m), roll(b, m), roll(strip, -67 - STRIP[t])
                    ta = ta + jnp.where(at >= m + 1, ra, rs)
                    tb = tb + jnp.where(at >= m, rb, ra)
                    el, er = el + rs, er + rb
            for tile, total in enumerate((el, ta, tb, er)):
                own[f, part, tile * LANES : (tile + 1) * LANES] = total

    def edge_sizes(sizes):
        for ti in range(ANG):
            spans = []
            for size in sizes:
                spans.append((view_of(ti, size), PAD + rows, PAD + rows + PAD))
                spans.append((view_of(ti, -size), 0, PAD))
            widen(ti, spans)
            for at in (-RING, 0, chunk, rows - 2 * chunk, rows - chunk, rows):
                ring = at < 0 or at >= rows
                part = slice(RING + at, RING + at + chunk)
                if ring and sizes == GROUPS[0]:
                    sums = [[None, None], [None, None]]
                else:
                    sums = [[acc[ti, f, h, part, :] for h in range(2)] for f in range(2)]
                middle = [cen[ti, h, part, :] for h in range(2)]
                for size in sizes:
                    for s in ((-size, size) if size else (0,)):
                        low, high = inner_rows(s)
                        if not low <= at < high:
                            view_step(view_of(ti, s), s, at, middle, sums)
                for f in range(2):
                    for h in range(2):
                        acc[ti, f, h, part, :] = sums[f][h]
        for size in sizes:
            if size == 0:
                packed_rows(HALF, 0, PAD)
                packed_rows(HALF, PAD + rows, full)
            else:
                packed_rows(HALF - size, 0, PAD)
                packed_rows(HALF + size, PAD + rows, full)
            for s in ((-size, size) if size else (0,)):
                low, high = inner_rows(s)
                packed_step(HALF + s, -RING, low)
                packed_step(HALF + s, high, rows + RING)

    combine(PAD, rows - PAD)
    for sizes in GROUPS:
        for size in sizes:
            if size:
                arrive(row_copies[2 * size : 2 * size + 2])
        edge_sizes(sizes)
    combine(-RING, PAD)
    combine(rows - PAD, rows + RING)

    inside = (gcol >= 0) & (gcol < ncol * cols) & (grow >= 0) & (grow < nrow * rows)
    coeff = damping + own[0] * (0.25 / VIEWS)
    field = own[1] * (-0.5 / VIEWS)
    diag = jnp.where(inside, coeff + weights, 1.0)
    zf = jnp.where(inside, field / diag, 0.0)
    inner = (slice(RING, RING + rows), slice(LANES, LANES + cols))
    source, zed = field[inner], zf[inner]

    def gather(z):
        return edge_e * east(z) + edge_w * west(z) + edge_s * south(z) + edge_n * north(z)

    around = gather(zf)
    yf = around / diag
    n1, y = around[inner], yf[inner]
    n2 = gather(yf)[inner]
    w = source - n1
    q = zed - y
    wv = n1 - n2
    v = w - wv
    sums = (y * n1, q * n1, q * w, y * wv, y * v, q * v)
    line = lax.broadcasted_iota(jnp.int32, (1, LANES), 1)
    packed = jnp.zeros((1, LANES), F32)
    for i, x in enumerate(sums):
        x = jnp.sum(x, axis=0, keepdims=True)
        x = jnp.sum(x, axis=1, keepdims=True)
        packed = jnp.where(line == i, x, packed)
    for step in range(5, len(rounds) + 1):
        learn(step)
    redout[0] = packed
    redbuf[me] = packed

    def red_copy(i):
        peer = (me + i) % count
        return pltpu.make_async_remote_copy(
            src_ref=redout.at[0], dst_ref=redbuf.at[me], send_sem=rsend.at[0], recv_sem=rrecv.at[0],
            device_id=(peer // ncol, peer % ncol), device_id_type=pl.DeviceIdType.MESH)

    def cast_out(i, carry):
        red_copy(i).start()
        return carry

    lax.fori_loop(1, count, cast_out, 0)
    drain(row_copies + side_copies + col_copies)
    others = redbuf.at[pl.ds(0, count - 1)]
    pltpu.make_async_copy(others, others, rrecv.at[0]).wait()
    pltpu.make_async_copy(others, others, rsend.at[0]).wait()
    totals = jnp.sum(redbuf[...], axis=0)
    f, g, h, k, l, m = [totals[:, i : i + 1] for i in range(6)]
    b, e = g + h, f + g
    delta = e / b
    step0 = (e + b) / b
    rz0 = e + b
    rz1 = f - 2.0 * delta * g + delta * delta * h
    wu1 = k - 2.0 * delta * l + delta * delta * m
    beta = rz1 / rz0
    step1 = rz1 / (wu1 - beta * rz1 / step0)
    direction = (y - delta * q) + beta * zed
    image = (wv - delta * v) + beta * w
    out[0] = step0 * zed + step1 * direction
    out[1] = (n1 - delta * w) - step1 * image


def solution(mesh):
    nrow, ncol = mesh.shape["row"], mesh.shape["col"]

    def shards(views):
        _, rows, cols = views.shape
        full = PAD + rows + PAD
        bf = views.dtype
        out = pl.pallas_call(
            functools.partial(kernel, nrow, ncol),
            out_shape=jax.ShapeDtypeStruct((2, rows, cols), F32),
            in_specs=[pl.BlockSpec(memory_space=pltpu.HBM)],
            out_specs=pl.BlockSpec(memory_space=pltpu.VMEM),
            scratch_shapes=[
                pltpu.VMEM((VIEWS, full, cols), bf),
                pltpu.VMEM((2, 5, rows, LANES), bf),
                pltpu.VMEM((5, full, LANES), bf),
                pltpu.VMEM((5, full, LANES), bf),
                pltpu.VMEM((full, LANES), bf),
                pltpu.VMEM((full, LANES), bf),
                pltpu.VMEM((VIEWS, 2, full + 2 * RING, LANES), F32),
                pltpu.VMEM((VIEWS, 2, full + 2 * RING, LANES), F32),
                pltpu.VMEM((ANG, cols, cols), bf),
                pltpu.VMEM((ANG, full + 2 * RING, LANES), F32),
                pltpu.VMEM((ANG, 2, rows + 2 * RING, LANES), F32),
                pltpu.VMEM((rows + 2 * RING, LANES), F32),
                pltpu.VMEM((ANG, 2, 2, rows + 2 * RING, LANES), F32),
                pltpu.VMEM((2, rows + 2 * RING, LANES), F32),
                pltpu.VMEM((2, rows + 2 * RING, cols + 2 * LANES), F32),
                pltpu.VMEM((nrow * ncol, 1, LANES), F32),
                pltpu.VMEM((1, 1, LANES), F32),
                pltpu.SemaphoreType.DMA((ANG,)),
                pltpu.SemaphoreType.DMA((22,)),
                pltpu.SemaphoreType.DMA((22,)),
                pltpu.SemaphoreType.DMA((1,)),
                pltpu.SemaphoreType.DMA((1,)),
                pltpu.SemaphoreType.REGULAR((8,)),
            ],
            compiler_params=pltpu.CompilerParams(collective_id=0, has_side_effects=True, vmem_limit_bytes=48 << 20),
        )(pltpu.with_memory_space_constraint(views, pltpu.HBM))
        return out[0], out[1]

    return jax.shard_map(
        shards,
        mesh=mesh,
        in_specs=(P(None, "row", "col"),),
        out_specs=(P("row", "col"), P("row", "col")),
        check_vma=False,
    )
```
